128 devices in a mesh: layer: 8 (over z, core), plane: 16 (over x, y).
Axes of the slice: x: 4, y: 4, z: 4, core: 2. Of those that a mesh axis runs over, the one named last changes fastest.
Arguments:
- right_sides: bfloat16 [64, 128, 2048], P('layer', None, 'plane'), may hold values from -6 to 6
- coupling: float32 [64, 2048], P('layer', 'plane'), may hold values from 0.84 to 0.98
- blocks: bfloat16 [64, 16, 23, 128, 128], P('layer', 'plane'), may hold values from -0.109375 to 0.109375
- block_index: int32 [64, 16, 23], P('layer', 'plane'), may hold values from 0 to 2
- section_lengths: int32 [8], P('layer'), may hold values from 1 to 8, as said below
Outputs:
- solution: bfloat16 [64, 128, 2048], P('layer', None, 'plane')
The draws below stay inside these ranges and needn't reach their ends.
Inputs may be any that keep to these rules, and one draw needn't show every extreme that they name: `section_lengths`: every section has at least one live layer, and some section has exactly 8.
All inputs are finite; a program needn't handle non-finite values.
Results may differ from the reference program's by a relative error of at most 0.04.
Values may be sent and summed in bfloat16 or wider, within the bound.
A program may use at most 64 MiB of HBM per device.

```python
import jax
import jax.numpy as jnp
from jax import lax

BLOCK = 128
COLS = 128
NNZ = 23
NB_DEV = 1
LMAX = 8
SLOTS = 64
NB = 16
NP = 2048
N_LAYER = 8


def draw_section_lengths(key, part):
    first_key = jax.random.fold_in(key, 11)
    second_key = jax.random.fold_in(key, 23)
    lengths = jax.random.randint(first_key, (N_LAYER,), 1, LMAX + 1).astype(jnp.int32)
    chosen = jax.random.randint(second_key, (), 0, N_LAYER).astype(jnp.int32)
    spots = jnp.arange(N_LAYER, dtype=jnp.int32)
    return jnp.where(spots == chosen, jnp.int32(LMAX), lengths).astype(jnp.int32)


def draw_coupling(key, part):
    coupling_key = jax.random.fold_in(key, 37)
    values = jax.random.uniform(coupling_key, (SLOTS, NP), jnp.float32, 0.84, 0.96)
    return values.astype(jnp.float32)


def place_ends(drawn, key, least, largest):
    shape = drawn.shape
    spot = [jax.random.randint(jax.random.fold_in(key, axis), (), 0, shape[axis]) for axis in range(len(shape))]
    drawn = drawn.at[tuple(spot)].set(least)
    longest = shape.index(max(shape))
    spot[longest] = (spot[longest] + 1) % shape[longest]
    return drawn.at[tuple(spot)].set(largest)


def steps_of(stream_key, shape, split, smallest, top_value):
    gain, own = 1.0, jax.random.fold_in(stream_key, 6)
    for dim, blocks in split:
        draws = jnp.exp(jax.random.uniform(jax.random.fold_in(own, dim), (blocks,), jnp.float32, smallest / len(split), top_value / len(split)))
        gain = gain * jnp.repeat(draws, shape[dim] // blocks).reshape([-1 if axis == dim else 1 for axis in range(len(shape))])
    return gain


def scatter_about(own_key, shape, spread, most, cuts=(), kind=jnp.bfloat16):
    array = jax.random.normal(own_key, shape, jnp.float32) * spread
    if len(cuts) > 0:
        array = steps_of(own_key, shape, cuts, -0.22, 0.18) * array
    return jnp.clip(array, min=-most, max=most).astype(kind)


def setup_inputs(seed: int = 0) -> dict:
    keys = jax.random.split(jax.random.key(seed), 6)
    return {
        "right_sides": scatter_about(keys[0], (SLOTS, COLS, NP), 1.0, 6.0, ((0, 8), (2, 16))),
        "coupling": draw_coupling(jax.random.fold_in(keys[5], 71), 0),
        "blocks": scatter_about(keys[2], (SLOTS, NB, NNZ, BLOCK, BLOCK), (NNZ * BLOCK) ** -0.5, 0.109375, ((0, 8), (1, 16))),
        "block_index": place_ends(jax.random.randint(keys[3], (SLOTS, NB, NNZ), 0, 3 * NB_DEV), jax.random.fold_in(keys[3], 1), 0, (3 * NB_DEV) - 1).astype(jnp.int32),
        "section_lengths": draw_section_lengths(jax.random.fold_in(keys[5], 71), 0),
    }


def apply_inverse(operand, blocks_layer, index_layer):
    columns = operand.shape[0]
    block_rows = index_layer.shape[0]
    block_size = blocks_layer.shape[-1]
    tile_rows = operand.reshape(columns, block_rows, block_size)
    zero_pad = jnp.zeros((columns, NB_DEV, block_size), operand.dtype)
    padded = jnp.concatenate([zero_pad, tile_rows, zero_pad], axis=1)
    row_base = (jnp.arange(block_rows, dtype=jnp.int32) // NB_DEV) * NB_DEV
    window_index = (row_base[:, None] + index_layer).astype(jnp.int32)
    picked = jnp.take(padded, window_index.reshape(-1), axis=1)
    picked = picked.reshape(columns, block_rows, index_layer.shape[1], block_size)
    result = jnp.einsum('citb,itab->cia', picked.astype(jnp.float32), blocks_layer.astype(jnp.float32))
    return result.reshape(columns, block_rows * block_size)


def reference(right_sides, coupling, blocks, block_index, section_lengths):
    slots = jnp.arange(SLOTS, dtype=jnp.int32)
    owner_dev = slots // LMAX
    position = slots % LMAX
    alive_slot = position < section_lengths[owner_dev]
    empty = jnp.zeros((COLS, NP), jnp.bfloat16)

    def down_step(previous, inputs):
        right_layer, couple_layer, blocks_layer, index_layer, alive = inputs

        def layer_work(carried):
            operand = (right_layer.astype(jnp.float32) + couple_layer[None, :] * carried.astype(jnp.float32)).astype(jnp.bfloat16)
            applied = apply_inverse(operand, blocks_layer, index_layer).astype(jnp.bfloat16)
            return applied, applied

        def layer_skip(carried):
            return carried, empty

        return lax.cond(alive, layer_work, layer_skip, previous)

    _, values = lax.scan(down_step, empty, (right_sides, coupling, blocks, block_index, alive_slot))

    def up_step(carried_in, inputs):
        value_layer, couple_layer, blocks_layer, index_layer, alive = inputs

        def layer_work(carried):
            summed = value_layer.astype(jnp.float32) + apply_inverse(carried, blocks_layer, index_layer)
            answer = summed.astype(jnp.bfloat16)
            passed = (couple_layer[None, :] * answer.astype(jnp.float32)).astype(jnp.bfloat16)
            return passed, answer

        def layer_skip(carried):
            return carried, empty

        return lax.cond(alive, layer_work, layer_skip, carried_in)

    _, solution = lax.scan(up_step, empty, (values, coupling, blocks, block_index, alive_slot), reverse=True)
    return solution
```

```python
import functools

import jax
import jax.numpy as jnp
from jax import lax
from jax.experimental import pallas as pl
from jax.experimental.pallas import tpu as pltpu
from jax.sharding import PartitionSpec as P

MESH = pl.DeviceIdType.MESH
BS = 128


def collapse_kernel(idx_ref, blocks_ref, out_ref, acc):
    level = pl.program_id(0)
    per_row = blocks_ref.shape[2]
    acc[...] = jnp.zeros_like(acc)

    def add(t, _):
        rows = pl.ds(pl.multiple_of(idx_ref[level * per_row + t] * BS, BS), BS)
        acc[rows, :] += blocks_ref[0, 0, t].astype(jnp.float32)
        return 0

    lax.fori_loop(0, per_row, add, 0)
    for b in range(3):
        out_ref[0, b * BS:(b + 1) * BS, :] = acc[b * BS:(b + 1) * BS, :].T.astype(out_ref.dtype)


def collapse(blocks, block_index):
    levels, _, per_row = block_index.shape
    return pl.pallas_call(
        collapse_kernel,
        grid_spec=pltpu.PrefetchScalarGridSpec(
            num_scalar_prefetch=1,
            grid=(levels,),
            in_specs=[pl.BlockSpec((1, 1, per_row, BS, BS), lambda l, idx: (l, 0, 0, 0, 0))],
            out_specs=pl.BlockSpec((1, 3 * BS, BS), lambda l, idx: (l, 0, 0)),
            scratch_shapes=[pltpu.VMEM((3 * BS, BS), jnp.float32)],
        ),
        out_shape=jax.ShapeDtypeStruct((levels, 3 * BS, BS), jnp.bfloat16),
        name="collapse",
    )(block_index.reshape(-1), blocks)


def sweep_kernel(len_ref, w_ref, r_ref, c_ref, o_ref,
                 xs, vals, cur, down_in, up_in, down_out, up_out, send_sem, recv_sem):
    rows, levels = w_ref.shape[0], w_ref.shape[1]
    width = rows * BS
    sections = lax.axis_size("layer")
    s = lax.axis_index("layer")
    live = len_ref[0]
    first, last = s == 0, s == sections - 1

    barrier = pltpu.get_barrier_semaphore()
    for near in (lax.rem(s + 1, sections), lax.rem(s + sections - 1, sections)):
        pl.semaphore_signal(barrier, inc=1, device_id={"layer": near}, device_id_type=MESH)
    pl.semaphore_wait(barrier, 2)

    def down_copy():
        return pltpu.make_async_remote_copy(
            src_ref=down_out, dst_ref=down_in, send_sem=send_sem.at[0], recv_sem=recv_sem.at[0],
            device_id={"layer": s + 1}, device_id_type=MESH)

    def up_copy():
        return pltpu.make_async_remote_copy(
            src_ref=up_out, dst_ref=up_in, send_sem=send_sem.at[1], recv_sem=recv_sem.at[1],
            device_id={"layer": s - 1}, device_id_type=MESH)

    xs[...] = jnp.zeros_like(xs)

    def apply(level):
        return [
            jnp.dot(xs[:, BS * i:BS * (i + 3)], w_ref[i, level], preferred_element_type=jnp.float32)
            for i in range(rows)
        ]

    @pl.when(first)
    def _():
        cur[...] = jnp.zeros_like(cur)

    @pl.when(jnp.logical_not(first))
    def _():
        down_copy().wait_recv()
        cur[...] = down_in[...].astype(jnp.float32)

    def down_level(level, _):
        alive = level < live
        operand = r_ref[level].astype(jnp.float32) + c_ref[level] * cur[...]
        xs[:, BS:BS + width] = operand.astype(jnp.bfloat16)
        for i, y in enumerate(apply(level)):
            cols = slice(BS * i, BS * (i + 1))
            value = y.astype(jnp.bfloat16)
            vals[level, :, cols] = value
            cur[:, cols] = jnp.where(alive, value.astype(jnp.float32), cur[:, cols])
        return 0

    lax.fori_loop(0, levels, down_level, 0)

    @pl.when(jnp.logical_not(last))
    def _():
        down_out[...] = cur[...].astype(jnp.bfloat16)
        down_copy().start()

    @pl.when(last)
    def _():
        xs[:, BS:BS + width] = jnp.zeros((xs.shape[0], width), jnp.bfloat16)

    @pl.when(jnp.logical_not(last))
    def _():
        up_copy().wait_recv()
        xs[:, BS:BS + width] = up_in[...]

    def up_level(step, _):
        level = levels - 1 - step
        alive = level < live
        for i, y in enumerate(apply(level)):
            cols = slice(BS * i, BS * (i + 1))
            wide = slice(BS * (i + 1), BS * (i + 2))
            answer = (vals[level, :, cols].astype(jnp.float32) + y).astype(jnp.bfloat16)
            o_ref[level, :, cols] = jnp.where(alive, answer, jnp.zeros_like(answer))
            passed = (c_ref[level, :, cols] * answer.astype(jnp.float32)).astype(jnp.bfloat16)
            cur[:, cols] = jnp.where(alive, passed, xs[:, wide]).astype(jnp.float32)
        xs[:, BS:BS + width] = cur[...].astype(jnp.bfloat16)
        return 0

    lax.fori_loop(0, levels, up_level, 0)

    @pl.when(jnp.logical_not(first))
    def _():
        up_out[...] = xs[:, BS:BS + width]
        up_copy().start()
        up_copy().wait_send()

    @pl.when(jnp.logical_not(last))
    def _():
        down_copy().wait_send()


def sweep(weights, right, coupling, lengths):
    levels, cols, width = right.shape
    vmem = pl.BlockSpec(memory_space=pltpu.VMEM)
    field = pltpu.VMEM((cols, width), jnp.bfloat16)
    return pl.pallas_call(
        sweep_kernel,
        in_specs=[pl.BlockSpec(memory_space=pltpu.SMEM), vmem, vmem, vmem],
        out_specs=vmem,
        out_shape=jax.ShapeDtypeStruct((levels, cols, width), jnp.bfloat16),
        scratch_shapes=[
            pltpu.VMEM((cols, width + 2 * BS), jnp.bfloat16),
            pltpu.VMEM((levels, cols, width), jnp.bfloat16),
            pltpu.VMEM((cols, width), jnp.float32),
            field, field, field, field,
            pltpu.SemaphoreType.DMA((2,)),
            pltpu.SemaphoreType.DMA((2,)),
        ],
        compiler_params=pltpu.CompilerParams(
            collective_id=0, has_side_effects=True, vmem_limit_bytes=48 * 1024 * 1024),
        name="sweep",
    )(lengths, weights, right, coupling)


def on_device(right_sides, coupling, blocks, block_index, section_lengths):
    own = collapse(blocks, block_index)
    weights = lax.all_gather(own, "plane", axis=0, tiled=False)
    right = lax.all_to_all(right_sides, "plane", split_axis=1, concat_axis=2, tiled=True)
    coupling = lax.all_gather(coupling, "plane", axis=1, tiled=True)[:, None, :]
    out = sweep(weights, right, coupling, section_lengths)
    return lax.all_to_all(out, "plane", split_axis=2, concat_axis=1, tiled=True)


def solution(mesh):
    return jax.shard_map(
        on_device,
        mesh=mesh,
        in_specs=(
            P("layer", None, "plane"),
            P("layer", "plane"),
            P("layer", "plane", None, None, None),
            P("layer", "plane", None),
            P("layer"),
        ),
        out_specs=P("layer", None, "plane"),
        check_vma=False,
    )
```

```python
import jax
import jax.numpy as jnp
from jax import lax
from jax.experimental import pallas as pl
from jax.experimental.pallas import tpu as pltpu
from jax.sharding import PartitionSpec as P

MESH = pl.DeviceIdType.MESH
BS = 128
SIDE = 4
LEVELS = 8
ROWS = SIDE * SIDE
PEERS = ROWS - 1


def sweep_kernel(len_ref, idx_ref, r_ref, c_ref, blocks_ref, o_ref,
                 raw, wall, r_all, c_all, o_all, xs, vals, cur, down_in, up_in, down_out, up_out,
                 raw_sem, g_send, g_recv, in_send, in_recv, out_send, out_recv, hop_send, hop_recv):
    sections = lax.axis_size("layer")
    s, me = lax.axis_index("layer"), lax.axis_index("plane")
    x, y = me // SIDE, lax.rem(me, SIDE)
    live = len_ref[0]
    first, last = s == 0, s == sections - 1
    per_row = raw.shape[1]

    loads = [pltpu.make_async_copy(blocks_ref.at[l, 0], raw.at[l], raw_sem.at[l]) for l in range(LEVELS)]
    for load in loads:
        load.start()

    def peer(d):
        return lax.rem(me + d, ROWS)

    barrier = pltpu.get_barrier_semaphore()
    for near in (lax.rem(s + 1, sections), lax.rem(s + sections - 1, sections)):
        pl.semaphore_signal(barrier, inc=1, device_id={"layer": near}, device_id_type=MESH)
    for d in range(1, ROWS):
        pl.semaphore_signal(barrier, inc=1, device_id={"plane": peer(d)}, device_id_type=MESH)

    def collapse(l):
        loads[l].wait()
        base = l * per_row
        picks = [[(idx_ref[base + t] == b).astype(jnp.float32) for b in range(3)] for t in range(per_row)]
        for b in range(3):
            total = raw[l, 0].astype(jnp.float32) * picks[0][b]
            for t in range(1, per_row):
                total += raw[l, t].astype(jnp.float32) * picks[t][b]
            wall[l, x, y, b * BS:(b + 1) * BS, :] = total.T.astype(jnp.bfloat16)

    def remote(src, dst, send, recv, **where):
        return pltpu.make_async_remote_copy(
            src_ref=src, dst_ref=dst, send_sem=send, recv_sem=recv, device_id=where, device_id_type=MESH)

    def at(dx, dy):
        return lax.rem(x + dx + SIDE, SIDE) * SIDE + lax.rem(y + dy + SIDE, SIDE)

    def near(axis, step):
        return at(step, 0) if axis == 0 else at(0, step)

    def shift(value, step):
        return lax.rem(value + step + SIDE, SIDE)

    half = 3 * BS // 2

    def own_send(l, step):
        slot = 0 if step == 1 else 1
        ref = wall.at[l, x, y]
        return remote(ref, ref, g_send.at[l, slot], g_recv.at[l, slot], plane=near(l % 2 == 0, step))

    def own_pass(l, step):
        slot = 2 if step == 1 else 3
        sx, sy = (x, shift(y, -step)) if l % 2 == 0 else (shift(x, -step), y)
        ref = wall.at[l, sx, sy, pl.ds(0 if step == 1 else half, half)]
        return remote(ref, ref, g_send.at[l, slot], g_recv.at[l, slot], plane=near(l % 2 == 0, step))

    def line_send(l, step):
        slot = 4 if step == 1 else 5
        ref = wall.at[l, x] if l % 2 == 0 else wall.at[l, :, y]
        return remote(ref, ref, g_send.at[l, slot], g_recv.at[l, slot], plane=near(l % 2 == 1, step))

    def line_pass(l, step):
        slot = 6 if step == 1 else 7
        part = pl.ds(0 if step == 1 else 2, 2)
        ref = wall.at[l, shift(x, -step), part] if l % 2 == 0 else wall.at[l, part, shift(y, -step)]
        return remote(ref, ref, g_send.at[l, slot], g_recv.at[l, slot], plane=near(l % 2 == 1, step))

    collapse(0)
    pl.semaphore_wait(barrier, 2 + PEERS)
    for d in range(1, ROWS):
        remote(c_ref, c_all.at[me], in_send.at[0], in_recv.at[0], plane=peer(d)).start()
    for l in range(LEVELS):
        if l > 0:
            collapse(l)
        for step in (1, -1):
            own_send(l, step).start()
        if l == 1:
            for d in range(1, ROWS):
                remote(r_ref.at[:, peer(d)], r_all.at[:, me], in_send.at[1], in_recv.at[1], plane=peer(d)).start()
    c_all[me] = c_ref[...]
    r_all[:, me] = r_ref[:, me]
    xs[...] = jnp.zeros_like(xs)

    for l in range(LEVELS):
        for step in (1, -1):
            own_send(l, step).wait_recv()
            own_pass(l, step).start()

    def lines(l):
        for step in (1, -1):
            own_pass(l, step).wait_recv()
        for step in (1, -1):
            line_send(l, step).start()

    def passes(l):
        for step in (1, -1):
            line_send(l, step).wait_recv()
            line_pass(l, step).start()

    for l in (0, 1, 2, 3):
        lines(l)
    for l in (0, 1):
        passes(l)
    for l in (4, 5):
        lines(l)
    for l in (2, 3):
        passes(l)
    for l in (6, 7):
        lines(l)
    for l in (4, 5, 6, 7):
        passes(l)

    others = c_all.at[pl.ds(0, PEERS)]
    pltpu.make_async_copy(others, others, in_recv.at[0]).wait()
    others = r_all.at[:, pl.ds(0, PEERS)]
    pltpu.make_async_copy(others, others, in_recv.at[1]).wait()

    def down_copy():
        return remote(down_out, down_in, hop_send.at[0], hop_recv.at[0], layer=s + 1)

    def up_copy():
        return remote(up_out, up_in, hop_send.at[1], hop_recv.at[1], layer=s - 1)

    def cols(i):
        return slice(BS * i, BS * (i + 1))

    def apply(l):
        return [
            jnp.dot(xs[:, BS * i:BS * (i + 3)], wall[l, i // SIDE, i % SIDE], preferred_element_type=jnp.float32)
            for i in range(ROWS)
        ]

    for l in range(LEVELS):
        for step in (1, -1):
            line_pass(l, step).wait_recv()

    @pl.when(first)
    def _():
        cur[...] = jnp.zeros_like(cur)

    @pl.when(jnp.logical_not(first))
    def _():
        down_copy().wait_recv()
        cur[...] = down_in[...].astype(jnp.float32)

    for l in range(LEVELS):
        alive = l < live
        for i in range(ROWS):
            operand = r_all[l, i].astype(jnp.float32) + c_all[i, l:l + 1] * cur[i]
            xs[:, cols(i + 1)] = operand.astype(jnp.bfloat16)
        for i, out in enumerate(apply(l)):
            value = out.astype(jnp.bfloat16)
            vals[l, i] = value
            cur[i] = jnp.where(alive, value.astype(jnp.float32), cur[i])

    @pl.when(jnp.logical_not(last))
    def _():
        down_out[...] = cur[...].astype(jnp.bfloat16)
        down_copy().start()
        up_copy_in = remote(up_out, up_in, hop_send.at[1], hop_recv.at[1], layer=s + 1)
        up_copy_in.wait_recv()
        cur[...] = up_in[...].astype(jnp.float32)

    @pl.when(last)
    def _():
        cur[...] = jnp.zeros_like(cur)

    def out_copy(l, d):
        return remote(o_all.at[l, peer(d)], o_ref.at[l, me], out_send, out_recv, plane=peer(d))

    for l in reversed(range(LEVELS)):
        alive = l < live
        for i in range(ROWS):
            xs[:, cols(i + 1)] = cur[i].astype(jnp.bfloat16)
        for i, out in enumerate(apply(l)):
            answer = (vals[l, i].astype(jnp.float32) + out).astype(jnp.bfloat16)
            o_all[l, i] = jnp.where(alive, answer, jnp.zeros_like(answer))
            passed = (c_all[i, l:l + 1] * answer.astype(jnp.float32)).astype(jnp.bfloat16)
            cur[i] = jnp.where(alive, passed.astype(jnp.float32), cur[i])
        if l == 0:
            @pl.when(jnp.logical_not(first))
            def _():
                up_out[...] = cur[...].astype(jnp.bfloat16)
                up_copy().start()
        for d in range(1, ROWS):
            out_copy(l, d).start()

    o_ref[:, me] = o_all[:, me]

    for l in range(LEVELS):
        for step in (1, -1):
            for send in (own_send, own_pass, line_send, line_pass):
                send(l, step).wait_send()
    others = c_all.at[pl.ds(0, PEERS)]
    pltpu.make_async_copy(others, others, in_send.at[0]).wait()
    others = r_all.at[:, pl.ds(0, PEERS)]
    pltpu.make_async_copy(others, others, in_send.at[1]).wait()

    @pl.when(jnp.logical_not(last))
    def _():
        down_copy().wait_send()

    @pl.when(jnp.logical_not(first))
    def _():
        up_copy().wait_send()

    others = o_all.at[:, pl.ds(0, PEERS)]
    pltpu.make_async_copy(others, others, out_send).wait()
    others = o_ref.at[:, pl.ds(0, PEERS)]
    pltpu.make_async_copy(others, others, out_recv).wait()


def sweep(lengths, index, right, coupling, blocks):
    levels, _, cols, _ = right.shape
    per_row = blocks.shape[2]
    vmem = pl.BlockSpec(memory_space=pltpu.VMEM)
    smem = pl.BlockSpec(memory_space=pltpu.SMEM)
    field = pltpu.VMEM((ROWS, cols, BS), jnp.bfloat16)
    stack = pltpu.VMEM((levels, ROWS, cols, BS), jnp.bfloat16)
    dma = pltpu.SemaphoreType.DMA
    return pl.pallas_call(
        sweep_kernel,
        in_specs=[smem, smem, vmem, vmem, pl.BlockSpec(memory_space=pl.ANY)],
        out_specs=vmem,
        out_shape=jax.ShapeDtypeStruct(right.shape, jnp.bfloat16),
        scratch_shapes=[
            pltpu.VMEM((levels, per_row, BS, BS), jnp.bfloat16),
            pltpu.VMEM((levels, SIDE, SIDE, 3 * BS, BS), jnp.bfloat16),
            stack,
            pltpu.VMEM((ROWS, levels, BS), jnp.float32),
            stack,
            pltpu.VMEM((cols, (ROWS + 2) * BS), jnp.bfloat16),
            stack,
            pltpu.VMEM((ROWS, cols, BS), jnp.float32),
            field, field, field, field,
            dma((levels,)), dma((levels, 8)), dma((levels, 8)),
            dma((2,)), dma((2,)), dma, dma, dma((2,)), dma((2,)),
        ],
        compiler_params=pltpu.CompilerParams(
            collective_id=0, has_side_effects=True, vmem_limit_bytes=48 * 1024 * 1024),
        name="sweep",
    )(lengths, index, right, coupling, blocks)


def on_device(right_sides, coupling, blocks, block_index, section_lengths):
    levels, columns, width = right_sides.shape
    right = right_sides.reshape(levels, ROWS, columns // ROWS, width)
    out = sweep(section_lengths, block_index.reshape(-1), right, coupling, blocks)
    return out.reshape(levels, columns, width)


def solution(mesh):
    return jax.shard_map(
        on_device,
        mesh=mesh,
        in_specs=(
            P("layer", None, "plane"),
            P("layer", "plane"),
            P("layer", "plane", None, None, None),
            P("layer", "plane", None),
            P("layer"),
        ),
        out_specs=P("layer", None, "plane"),
        check_vma=False,
    )
```

```python
import jax
import jax.numpy as jnp
from jax import lax
from jax.experimental import pallas as pl
from jax.experimental.pallas import tpu as pltpu
from jax.sharding import PartitionSpec as P

MESH = pl.DeviceIdType.MESH
BS = 128
SIDE = 4
LEVELS = 8
ROWS = SIDE * SIDE
PEERS = ROWS - 1


def sweep_kernel(len_ref, idx_ref, r_ref, c_ref, blocks_ref, o_ref,
                 raw, wall, r_all, c_all, o_all, right, couple, vals, cur, down_in, up_in, down_out, up_out,
                 raw_sem, own_sem, g_send, g_recv, in_send, in_recv, out_send, out_recv, hop_send, hop_recv):
    sections = lax.axis_size("layer")
    s, me = lax.axis_index("layer"), lax.axis_index("plane")
    x, y = me // SIDE, lax.rem(me, SIDE)
    live = len_ref[0]
    first, last = s == 0, s == sections - 1
    per_row = raw.shape[1]

    keep_c = pltpu.make_async_copy(c_ref, c_all.at[me], own_sem.at[0])
    keep_r = pltpu.make_async_copy(r_ref.at[:, me], r_all.at[:, me], own_sem.at[1])
    keep_c.start()
    keep_r.start()
    loads = [pltpu.make_async_copy(blocks_ref.at[l, 0], raw.at[l], raw_sem.at[l]) for l in range(LEVELS)]
    for load in loads:
        load.start()

    def peer(d):
        return lax.rem(me + d, ROWS)

    barrier = pltpu.get_barrier_semaphore()
    for near in (lax.rem(s + 1, sections), lax.rem(s + sections - 1, sections)):
        pl.semaphore_signal(barrier, inc=1, device_id={"layer": near}, device_id_type=MESH)
    for d in range(1, ROWS):
        pl.semaphore_signal(barrier, inc=1, device_id={"plane": peer(d)}, device_id_type=MESH)

    def collapse(l):
        loads[l].wait()
        picks = [[(idx_ref[l, 0, t] == b).astype(jnp.float32) for b in range(3)] for t in range(per_row)]
        for b in range(3):
            total = raw[l, 0].astype(jnp.float32) * picks[0][b]
            for t in range(1, per_row):
                total += raw[l, t].astype(jnp.float32) * picks[t][b]
            wall[l, x, y, b * BS:(b + 1) * BS, :] = total.T.astype(jnp.bfloat16)

    def remote(src, dst, send, recv, **where):
        return pltpu.make_async_remote_copy(
            src_ref=src, dst_ref=dst, send_sem=send, recv_sem=recv, device_id=where, device_id_type=MESH)

    def at(dx, dy):
        return lax.rem(x + dx + SIDE, SIDE) * SIDE + lax.rem(y + dy + SIDE, SIDE)

    def near(axis, step):
        return at(step, 0) if axis == 0 else at(0, step)

    def shift(value, step):
        return lax.rem(value + step + SIDE, SIDE)

    half = 3 * BS // 2

    def own_send(l, step):
        slot = 0 if step == 1 else 1
        ref = wall.at[l, x, y]
        return remote(ref, ref, g_send.at[l, slot], g_recv.at[l, slot], plane=near(l % 2 == 0, step))

    def own_pass(l, step):
        slot = 2 if step == 1 else 3
        sx, sy = (x, shift(y, -step)) if l % 2 == 0 else (shift(x, -step), y)
        ref = wall.at[l, sx, sy, pl.ds(0 if step == 1 else half, half)]
        return remote(ref, ref, g_send.at[l, slot], g_recv.at[l, slot], plane=near(l % 2 == 0, step))

    def line_send(l, step):
        slot = 4 if step == 1 else 5
        ref = wall.at[l, x] if l % 2 == 0 else wall.at[l, :, y]
        return remote(ref, ref, g_send.at[l, slot], g_recv.at[l, slot], plane=near(l % 2 == 1, step))

    def line_pass(l, step):
        slot = 6 if step == 1 else 7
        part = pl.ds(0 if step == 1 else 2, 2)
        ref = wall.at[l, shift(x, -step), part] if l % 2 == 0 else wall.at[l, part, shift(y, -step)]
        return remote(ref, ref, g_send.at[l, slot], g_recv.at[l, slot], plane=near(l % 2 == 1, step))

    collapse(0)
    pl.semaphore_wait(barrier, 2 + PEERS)
    for d in range(1, ROWS):
        remote(c_ref, c_all.at[me], in_send.at[0], in_recv.at[0], plane=peer(d)).start()
    for l in range(LEVELS):
        if l > 0:
            collapse(l)
        for step in (1, -1):
            own_send(l, step).start()
        if l == 1:
            for d in range(1, ROWS):
                remote(r_ref.at[:, peer(d)], r_all.at[:, me], in_send.at[1], in_recv.at[1], plane=peer(d)).start()

    for l in range(LEVELS):
        for step in (1, -1):
            own_send(l, step).wait_recv()
            own_pass(l, step).start()

    def lines(l):
        for step in (1, -1):
            own_pass(l, step).wait_recv()
        for step in (1, -1):
            line_send(l, step).start()

    def passes(l):
        for step in (1, -1):
            line_send(l, step).wait_recv()
            line_pass(l, step).start()

    for l in (0, 1, 2, 3):
        lines(l)
    for l in (0, 1):
        passes(l)
    for l in (4, 5):
        lines(l)
    for l in (2, 3):
        passes(l)
    for l in (6, 7):
        lines(l)
    keep_c.wait()
    keep_r.wait()
    others = c_all.at[pl.ds(0, PEERS)]
    pltpu.make_async_copy(others, others, in_recv.at[0]).wait()
    others = r_all.at[:, pl.ds(0, PEERS)]
    pltpu.make_async_copy(others, others, in_recv.at[1]).wait()
    for i in range(ROWS):
        for l in range(LEVELS):
            right[l, i] = r_all[l, i].astype(jnp.float32)
            couple[l, i] = jnp.broadcast_to(c_all[i, l:l + 1], couple.shape[2:])
    for l in (4, 5, 6, 7):
        passes(l)

    def down_copy():
        return remote(down_out, down_in, hop_send.at[0], hop_recv.at[0], layer=s + 1)

    def up_copy():
        return remote(up_out, up_in, hop_send.at[1], hop_recv.at[1], layer=s - 1)

    def apply(l, tiles):
        edge = jnp.zeros(cur.shape[1:], jnp.bfloat16)
        padded = [edge] + [tile.astype(jnp.bfloat16) for tile in tiles] + [edge]
        return [
            jnp.dot(jnp.concatenate(padded[i:i + 3], axis=1), wall[l, i // SIDE, i % SIDE],
                    preferred_element_type=jnp.float32)
            for i in range(ROWS)
        ]

    def alive(l):
        return jnp.full(cur.shape[1:], live, jnp.int32) > l

    for l in range(LEVELS):
        for step in (1, -1):
            line_pass(l, step).wait_recv()

    @pl.when(first)
    def _():
        cur[...] = jnp.zeros_like(cur)

    @pl.when(jnp.logical_not(first))
    def _():
        down_copy().wait_recv()
        cur[...] = down_in[...].astype(jnp.float32)

    now = [cur[i] for i in range(ROWS)]
    for l in range(LEVELS):
        keep = alive(l)
        values = apply(l, [right[l, i] + couple[l, i] * now[i] for i in range(ROWS)])
        for i in range(ROWS):
            vals[l, i] = values[i]
        now = [jnp.where(keep, values[i], now[i]) for i in range(ROWS)]
    for i in range(ROWS):
        down_out[i] = now[i].astype(jnp.bfloat16)

    @pl.when(jnp.logical_not(last))
    def _():
        down_copy().start()
        up_copy_in = remote(up_out, up_in, hop_send.at[1], hop_recv.at[1], layer=s + 1)
        up_copy_in.wait_recv()
        cur[...] = up_in[...].astype(jnp.float32)

    @pl.when(last)
    def _():
        cur[...] = jnp.zeros_like(cur)

    def out_copy(d):
        return remote(o_all.at[:, peer(d)], o_ref.at[:, me], out_send, out_recv, plane=peer(d))

    now = [cur[i] for i in range(ROWS)]
    for l in reversed(range(LEVELS)):
        keep = alive(l)
        sums = apply(l, now)
        answers = [vals[l, i] + sums[i] for i in range(ROWS)]
        now = [jnp.where(keep, couple[l, i] * answers[i], now[i]) for i in range(ROWS)]
        if l == 0:
            for i in range(ROWS):
                up_out[i] = now[i].astype(jnp.bfloat16)

            @pl.when(jnp.logical_not(first))
            def _():
                up_copy().start()
        for i in range(ROWS):
            o_all[l, i] = jnp.where(keep, answers[i], 0.0).astype(jnp.bfloat16)

    for d in range(1, ROWS):
        out_copy(d).start()
    o_ref[:, me] = o_all[:, me]

    for l in range(LEVELS):
        for step in (1, -1):
            for send in (own_send, own_pass, line_send, line_pass):
                send(l, step).wait_send()
    others = c_all.at[pl.ds(0, PEERS)]
    pltpu.make_async_copy(others, others, in_send.at[0]).wait()
    others = r_all.at[:, pl.ds(0, PEERS)]
    pltpu.make_async_copy(others, others, in_send.at[1]).wait()

    @pl.when(jnp.logical_not(last))
    def _():
        down_copy().wait_send()

    @pl.when(jnp.logical_not(first))
    def _():
        up_copy().wait_send()

    others = o_all.at[:, pl.ds(0, PEERS)]
    pltpu.make_async_copy(others, others, out_send).wait()
    others = o_ref.at[:, pl.ds(0, PEERS)]
    pltpu.make_async_copy(others, others, out_recv).wait()


def sweep(lengths, index, right, coupling, blocks):
    levels, _, cols, _ = right.shape
    per_row = blocks.shape[2]
    vmem = pl.BlockSpec(memory_space=pltpu.VMEM)
    smem = pl.BlockSpec(memory_space=pltpu.SMEM)
    hbm = pl.BlockSpec(memory_space=pl.ANY)
    field = pltpu.VMEM((ROWS, cols, BS), jnp.bfloat16)
    stack = pltpu.VMEM((levels, ROWS, cols, BS), jnp.bfloat16)
    wide = pltpu.VMEM((levels, ROWS, cols, BS), jnp.float32)
    dma = pltpu.SemaphoreType.DMA
    return pl.pallas_call(
        sweep_kernel,
        in_specs=[smem, smem, hbm, hbm, hbm],
        out_specs=vmem,
        out_shape=jax.ShapeDtypeStruct(right.shape, jnp.bfloat16),
        scratch_shapes=[
            pltpu.VMEM((levels, per_row, BS, BS), jnp.bfloat16),
            pltpu.VMEM((levels, SIDE, SIDE, 3 * BS, BS), jnp.bfloat16),
            stack,
            pltpu.VMEM((ROWS, levels, BS), jnp.float32),
            stack,
            wide, wide, wide,
            pltpu.VMEM((ROWS, cols, BS), jnp.float32),
            field, field, field, field,
            dma((levels,)), dma((2,)), dma((levels, 8)), dma((levels, 8)),
            dma((2,)), dma((2,)), dma, dma, dma((2,)), dma((2,)),
        ],
        compiler_params=pltpu.CompilerParams(
            collective_id=0, has_side_effects=True, vmem_limit_bytes=60 * 1024 * 1024),
        name="sweep",
    )(lengths, index, right, coupling, blocks)


def on_device(right_sides, coupling, blocks, block_index, section_lengths):
    levels, columns, width = right_sides.shape
    right = right_sides.reshape(levels, ROWS, columns // ROWS, width)
    out = sweep(section_lengths, block_index, right, coupling, blocks)
    return out.reshape(levels, columns, width)


def solution(mesh):
    return jax.shard_map(
        on_device,
        mesh=mesh,
        in_specs=(
            P("layer", None, "plane"),
            P("layer", "plane"),
            P("layer", "plane", None, None, None),
            P("layer", "plane", None),
            P("layer"),
        ),
        out_specs=P("layer", None, "plane"),
        check_vma=False,
    )
```

```python
import jax
import jax.numpy as jnp
from jax import lax
from jax.experimental import pallas as pl
from jax.experimental.pallas import tpu as pltpu
from jax.sharding import PartitionSpec as P

MESH = pl.DeviceIdType.MESH
BS = 128
SIDE = 4
LEVELS = 8
ROWS = SIDE * SIDE
PEERS = ROWS - 1
CHUNK = 4


def sweep_kernel(len_ref, idx_ref, r_ref, c_ref, blocks_ref, o_ref,
                 raw, wall, r_all, c_all, o_all, right, couple, vals, down_in, up_in, down_out, up_out,
                 raw_sem, own_sem, g_send, g_recv, in_send, in_recv, out_send, out_recv, hop_send, hop_recv):
    sections = lax.axis_size("layer")
    s, me = lax.axis_index("layer"), lax.axis_index("plane")
    x, y = me // SIDE, lax.rem(me, SIDE)
    live = len_ref[0]
    first, last = s == 0, s == sections - 1
    per_row = raw.shape[1]

    keep_c = pltpu.make_async_copy(c_ref, c_all.at[me], own_sem.at[0])
    keep_r = pltpu.make_async_copy(r_ref.at[:, me], r_all.at[:, me], own_sem.at[1])
    keep_c.start()
    keep_r.start()
    loads = [pltpu.make_async_copy(blocks_ref.at[l, 0], raw.at[l], raw_sem.at[l]) for l in range(LEVELS)]
    for load in loads:
        load.start()

    def peer(d):
        return lax.rem(me + d, ROWS)

    barrier = pltpu.get_barrier_semaphore()
    for near in (lax.rem(s + 1, sections), lax.rem(s + sections - 1, sections)):
        pl.semaphore_signal(barrier, inc=1, device_id={"layer": near}, device_id_type=MESH)
    for d in range(1, ROWS):
        pl.semaphore_signal(barrier, inc=1, device_id={"plane": peer(d)}, device_id_type=MESH)

    def collapse(l):
        loads[l].wait()
        picks = [[(idx_ref[l, 0, t] == b).astype(jnp.float32) for b in range(3)] for t in range(per_row)]
        for b in range(3):
            total = raw[l, 0].astype(jnp.float32) * picks[0][b]
            for t in range(1, per_row):
                total += raw[l, t].astype(jnp.float32) * picks[t][b]
            wall[l, x, y, b * BS:(b + 1) * BS, :] = total.T.astype(jnp.bfloat16)

    def remote(src, dst, send, recv, **where):
        return pltpu.make_async_remote_copy(
            src_ref=src, dst_ref=dst, send_sem=send, recv_sem=recv, device_id=where, device_id_type=MESH)

    def at(dx, dy):
        return lax.rem(x + dx + SIDE, SIDE) * SIDE + lax.rem(y + dy + SIDE, SIDE)

    def near(axis, step):
        return at(step, 0) if axis == 0 else at(0, step)

    def shift(value, step):
        return lax.rem(value + step + SIDE, SIDE)

    half = 3 * BS // 2

    def own_send(l, step):
        slot = 0 if step == 1 else 1
        ref = wall.at[l, x, y]
        return remote(ref, ref, g_send.at[l, slot], g_recv.at[l, slot], plane=near(l % 2 == 0, step))

    def own_pass(l, step):
        slot = 2 if step == 1 else 3
        sx, sy = (x, shift(y, -step)) if l % 2 == 0 else (shift(x, -step), y)
        ref = wall.at[l, sx, sy, pl.ds(0 if step == 1 else half, half)]
        return remote(ref, ref, g_send.at[l, slot], g_recv.at[l, slot], plane=near(l % 2 == 0, step))

    def line_send(l, step):
        slot = 4 if step == 1 else 5
        ref = wall.at[l, x] if l % 2 == 0 else wall.at[l, :, y]
        return remote(ref, ref, g_send.at[l, slot], g_recv.at[l, slot], plane=near(l % 2 == 1, step))

    def line_pass(l, step):
        slot = 6 if step == 1 else 7
        part = pl.ds(0 if step == 1 else 2, 2)
        ref = wall.at[l, shift(x, -step), part] if l % 2 == 0 else wall.at[l, part, shift(y, -step)]
        return remote(ref, ref, g_send.at[l, slot], g_recv.at[l, slot], plane=near(l % 2 == 1, step))

    collapse(0)
    pl.semaphore_wait(barrier, 2 + PEERS)
    for d in range(1, ROWS):
        remote(c_ref, c_all.at[me], in_send.at[0], in_recv.at[0], plane=peer(d)).start()
    for l in range(LEVELS):
        if l > 0:
            collapse(l)
        for step in (1, -1):
            own_send(l, step).start()
        if l == 1:
            for d in range(1, ROWS):
                remote(r_ref.at[:, peer(d)], r_all.at[:, me], in_send.at[1], in_recv.at[1], plane=peer(d)).start()

    for l in range(LEVELS):
        for step in (1, -1):
            own_send(l, step).wait_recv()
            own_pass(l, step).start()

    def lines(l):
        for step in (1, -1):
            own_pass(l, step).wait_recv()
        for step in (1, -1):
            line_send(l, step).start()

    def passes(l):
        for step in (1, -1):
            line_send(l, step).wait_recv()
            line_pass(l, step).start()

    for l in (0, 1, 2, 3):
        lines(l)
    for l in (0, 1):
        passes(l)
    for l in (4, 5):
        lines(l)
    for l in (2, 3):
        passes(l)
    for l in (6, 7):
        lines(l)
    keep_c.wait()
    keep_r.wait()
    others = c_all.at[pl.ds(0, PEERS)]
    pltpu.make_async_copy(others, others, in_recv.at[0]).wait()
    others = r_all.at[:, pl.ds(0, PEERS)]
    pltpu.make_async_copy(others, others, in_recv.at[1]).wait()
    for i in range(ROWS):
        for l in range(LEVELS):
            right[l, i] = r_all[l, i].astype(jnp.float32)
            couple[l, i] = jnp.broadcast_to(c_all[i, l:l + 1], couple.shape[2:])
    for l in (4, 5, 6, 7):
        passes(l)

    tile = r_all.shape[2:]

    def pair(l, i, field):
        zero = jnp.zeros(tile, jnp.float32)
        before, here, there, after = [field(j) if 0 <= j < ROWS else zero for j in range(i - 1, i + 3)]
        left, right_ = wall.at[l, i // SIDE, i % SIDE], wall.at[l, (i + 1) // SIDE, (i + 1) % SIDE]
        centre = jnp.dot(
            jnp.concatenate([here, there], axis=1).astype(jnp.bfloat16),
            jnp.concatenate([left[BS:], right_[:2 * BS]], axis=1),
            preferred_element_type=jnp.float32)
        outer = jnp.concatenate(
            [jnp.concatenate([before, zero], axis=0), jnp.concatenate([zero, after], axis=0)], axis=1)
        outer = jnp.dot(
            outer.astype(jnp.bfloat16), jnp.concatenate([left[:BS], right_[2 * BS:]], axis=0),
            preferred_element_type=jnp.float32)
        half_ = tile[0]
        return centre[:, :BS] + outer[:half_], centre[:, BS:] + outer[half_:]

    def alive(l):
        return jnp.full(tile, live, jnp.int32) > l

    def chunk(ref, part):
        return ref.at[pl.ds(CHUNK * part, CHUNK)]

    def down_copy(part, where):
        return remote(chunk(down_out, part), chunk(down_in, part), hop_send.at[0, part], hop_recv.at[0, part], layer=where)

    def up_copy(part, where):
        return remote(chunk(up_out, part), chunk(up_in, part), hop_send.at[1, part], hop_recv.at[1, part], layer=where)

    def arrivals(copy, where, i):
        if i == 0:
            copy(0, where).wait_recv()
        part = (i + 2) // CHUNK
        if (i + 2) % CHUNK == 0 and part < ROWS // CHUNK:
            copy(part, where).wait_recv()

    def arrived(l):
        for step in (1, -1):
            line_pass(l, step).wait_recv()

    def down(start):
        now = {}

        def operand(l, i):
            if l > 0:
                return right[l, i] + couple[l, i] * now[l - 1, i]
            if start:
                return right[l, i]
            return right[l, i] + couple[l, i] * down_in[i].astype(jnp.float32)

        for l in range(LEVELS):
            if start:
                arrived(l)
            keep = alive(l)
            made = {}

            def field(i):
                if i not in made:
                    made[i] = operand(l, i)
                return made[i]

            for i in range(0, ROWS, 2):
                if l == 0 and not start:
                    arrivals(down_copy, s - 1, i)
                for j, value in zip((i, i + 1), pair(l, i, field)):
                    vals[l, j] = value
                    if l > 0:
                        value = jnp.where(keep, value, now[l - 1, j])
                    now[l, j] = value
                if l == LEVELS - 1:
                    for j in (i, i + 1):
                        down_out[j] = now[l, j].astype(jnp.bfloat16)
                    if (i + 2) % CHUNK == 0:
                        if start:
                            down_copy(i // CHUNK, s + 1).start()
                        else:
                            @pl.when(jnp.logical_not(last))
                            def _(part=i // CHUNK):
                                down_copy(part, s + 1).start()

    def out_copy(d, low, high):
        part = pl.ds(low, high - low)
        return remote(o_all.at[part, peer(d)], o_ref.at[part, me], out_send, out_recv, plane=peer(d))

    def out_sends(low, high):
        for d in range(1, ROWS):
            out_copy(d, low, high).start()

    def up(start, end):
        now = {}

        def field_at(l, i):
            return now[l + 1, i] if l < LEVELS - 1 else up_in[i].astype(jnp.float32)

        for l in reversed(range(LEVELS)):
            keep = alive(l)
            top = l == LEVELS - 1
            for i in range(0, ROWS, 2):
                if start and top:
                    sums = (0.0, 0.0)
                else:
                    if top:
                        arrivals(up_copy, s + 1, i)
                    sums = pair(l, i, lambda j: field_at(l, j))
                for j, total in zip((i, i + 1), sums):
                    answer = vals[l, j] + total
                    o_all[l, j] = jnp.where(keep, answer, 0.0).astype(jnp.bfloat16)
                    if l > 0 or not end:
                        behind = jnp.zeros(tile, jnp.float32) if start and top else field_at(l, j)
                        now[l, j] = jnp.where(keep, couple[l, j] * answer, behind)
                if l == 0 and not end:
                    for j in (i, i + 1):
                        up_out[j] = now[l, j].astype(jnp.bfloat16)
                    if (i + 2) % CHUNK == 0:
                        up_copy(i // CHUNK, s - 1).start()
            if end and l == 4:
                out_sends(4, 8)
            if end and l == 1:
                out_sends(1, 4)
        if end:
            out_sends(0, 1)
        else:
            out_sends(0, LEVELS)

    @pl.when(first)
    def _():
        down(True)

    @pl.when(jnp.logical_not(first))
    def _():
        for l in range(LEVELS):
            arrived(l)
        down(False)

    @pl.when(last)
    def _():
        up(True, False)

    @pl.when(jnp.logical_and(jnp.logical_not(first), jnp.logical_not(last)))
    def _():
        up(False, False)

    @pl.when(first)
    def _():
        up(False, True)

    o_ref[:, me] = o_all[:, me]

    for l in range(LEVELS):
        for step in (1, -1):
            for send in (own_send, own_pass, line_send, line_pass):
                send(l, step).wait_send()
    others = c_all.at[pl.ds(0, PEERS)]
    pltpu.make_async_copy(others, others, in_send.at[0]).wait()
    others = r_all.at[:, pl.ds(0, PEERS)]
    pltpu.make_async_copy(others, others, in_send.at[1]).wait()

    @pl.when(jnp.logical_not(last))
    def _():
        for part in range(ROWS // CHUNK):
            down_copy(part, s + 1).wait_send()

    @pl.when(jnp.logical_not(first))
    def _():
        for part in range(ROWS // CHUNK):
            up_copy(part, s - 1).wait_send()

    others = o_all.at[:, pl.ds(0, PEERS)]
    pltpu.make_async_copy(others, others, out_send).wait()
    others = o_ref.at[:, pl.ds(0, PEERS)]
    pltpu.make_async_copy(others, others, out_recv).wait()


def sweep(lengths, index, right, coupling, blocks):
    levels, _, cols, _ = right.shape
    per_row = blocks.shape[2]
    vmem = pl.BlockSpec(memory_space=pltpu.VMEM)
    smem = pl.BlockSpec(memory_space=pltpu.SMEM)
    hbm = pl.BlockSpec(memory_space=pl.ANY)
    field = pltpu.VMEM((ROWS, cols, BS), jnp.bfloat16)
    stack = pltpu.VMEM((levels, ROWS, cols, BS), jnp.bfloat16)
    wide = pltpu.VMEM((levels, ROWS, cols, BS), jnp.float32)
    dma = pltpu.SemaphoreType.DMA
    return pl.pallas_call(
        sweep_kernel,
        in_specs=[smem, smem, hbm, hbm, hbm],
        out_specs=vmem,
        out_shape=jax.ShapeDtypeStruct(right.shape, jnp.bfloat16),
        scratch_shapes=[
            pltpu.VMEM((levels, per_row, BS, BS), jnp.bfloat16),
            pltpu.VMEM((levels, SIDE, SIDE, 3 * BS, BS), jnp.bfloat16),
            stack,
            pltpu.VMEM((ROWS, levels, BS), jnp.float32),
            stack,
            wide, wide, wide,
            field, field, field, field,
            dma((levels,)), dma((2,)), dma((levels, 8)), dma((levels, 8)),
            dma((2,)), dma((2,)), dma, dma, dma((2, ROWS // CHUNK)), dma((2, ROWS // CHUNK)),
        ],
        compiler_params=pltpu.CompilerParams(
            collective_id=0, has_side_effects=True, vmem_limit_bytes=60 * 1024 * 1024),
        name="sweep",
    )(lengths, index, right, coupling, blocks)


def on_device(right_sides, coupling, blocks, block_index, section_lengths):
    levels, columns, width = right_sides.shape
    right = right_sides.reshape(levels, ROWS, columns // ROWS, width)
    out = sweep(section_lengths, block_index, right, coupling, blocks)
    return out.reshape(levels, columns, width)


def solution(mesh):
    return jax.shard_map(
        on_device,
        mesh=mesh,
        in_specs=(
            P("layer", None, "plane"),
            P("layer", "plane"),
            P("layer", "plane", None, None, None),
            P("layer", "plane", None),
            P("layer"),
        ),
        out_specs=P("layer", None, "plane"),
        check_vma=False,
    )
```

```python
import jax
import jax.numpy as jnp
from jax import lax
from jax.experimental import pallas as pl
from jax.experimental.pallas import tpu as pltpu
from jax.sharding import PartitionSpec as P

MESH = pl.DeviceIdType.MESH
BS = 128
SIDE = 4
LEVELS = 8
ROWS = SIDE * SIDE
PEERS = ROWS - 1
CHUNK = 16


def sweep_kernel(len_ref, idx_ref, r_ref, c_ref, blocks_ref, o_ref,
                 raw, wall, r_all, c_all, o_all, right, couple, vals, down_in, up_in, down_out, up_out,
                 raw_sem, own_sem, g_send, g_recv, in_send, in_recv, out_send, out_recv, hop_send, hop_recv, rounds):
    sections = lax.axis_size("layer")
    s, me = lax.axis_index("layer"), lax.axis_index("plane")
    x, y = me // SIDE, lax.rem(me, SIDE)
    live = len_ref[0]
    first, last = s == 0, s == sections - 1
    per_row = raw.shape[1]

    keep_c = pltpu.make_async_copy(c_ref, c_all.at[me], own_sem.at[0])
    keep_r = pltpu.make_async_copy(r_ref.at[:, me], r_all.at[:, me], own_sem.at[1])
    keep_c.start()
    keep_r.start()
    loads = [pltpu.make_async_copy(blocks_ref.at[l, 0], raw.at[l], raw_sem.at[l]) for l in range(LEVELS)]
    for load in loads:
        load.start()

    def peer(d):
        return lax.rem(me + d, ROWS)

    barrier = pltpu.get_barrier_semaphore()
    for near in (lax.rem(s + 1, sections), lax.rem(s + sections - 1, sections)):
        pl.semaphore_signal(barrier, inc=1, device_id={"layer": near}, device_id_type=MESH)
    def at(dx, dy):
        return lax.rem(x + dx + SIDE, SIDE) * SIDE + lax.rem(y + dy + SIDE, SIDE)

    beside = [at(1, 0), at(-1, 0), at(0, 1), at(0, -1)]
    for near in beside:
        pl.semaphore_signal(barrier, inc=1, device_id={"plane": near}, device_id_type=MESH)

    def spread(turn):
        for near in beside:
            pl.semaphore_signal(rounds.at[turn], inc=1, device_id={"plane": near}, device_id_type=MESH)
        pl.semaphore_wait(rounds.at[turn], len(beside))

    def collapse(l):
        loads[l].wait()
        picks = [[(idx_ref[l, 0, t] == b).astype(jnp.float32) for b in range(3)] for t in range(per_row)]
        for b in range(3):
            total = raw[l, 0].astype(jnp.float32) * picks[0][b]
            for t in range(1, per_row):
                total += raw[l, t].astype(jnp.float32) * picks[t][b]
            wall[l, x, y, b * BS:(b + 1) * BS, :] = total.T.astype(jnp.bfloat16)

    def remote(src, dst, send, recv, **where):
        return pltpu.make_async_remote_copy(
            src_ref=src, dst_ref=dst, send_sem=send, recv_sem=recv, device_id=where, device_id_type=MESH)

    def near(axis, step):
        return at(step, 0) if axis == 0 else at(0, step)

    def shift(value, step):
        return lax.rem(value + step + SIDE, SIDE)

    half = 3 * BS // 2

    def own_send(l, step):
        slot = 0 if step == 1 else 1
        ref = wall.at[l, x, y]
        return remote(ref, ref, g_send.at[l, slot], g_recv.at[l, slot], plane=near(l % 2 == 0, step))

    def own_pass(l, step):
        slot = 2 if step == 1 else 3
        sx, sy = (x, shift(y, -step)) if l % 2 == 0 else (shift(x, -step), y)
        ref = wall.at[l, sx, sy, pl.ds(0 if step == 1 else half, half)]
        return remote(ref, ref, g_send.at[l, slot], g_recv.at[l, slot], plane=near(l % 2 == 0, step))

    def line_send(l, step):
        slot = 4 if step == 1 else 5
        ref = wall.at[l, x] if l % 2 == 0 else wall.at[l, :, y]
        return remote(ref, ref, g_send.at[l, slot], g_recv.at[l, slot], plane=near(l % 2 == 1, step))

    def line_pass(l, step):
        slot = 6 if step == 1 else 7
        part = pl.ds(0 if step == 1 else 2, 2)
        ref = wall.at[l, shift(x, -step), part] if l % 2 == 0 else wall.at[l, part, shift(y, -step)]
        return remote(ref, ref, g_send.at[l, slot], g_recv.at[l, slot], plane=near(l % 2 == 1, step))

    collapse(0)
    pl.semaphore_wait(barrier, 2 + len(beside))
    for l in range(LEVELS):
        if l > 0:
            collapse(l)
        for step in (1, -1):
            own_send(l, step).start()
        if l in (1, 3, 5):
            spread(l // 2)
    for d in range(1, ROWS):
        remote(c_ref, c_all.at[me], in_send.at[0], in_recv.at[0], plane=peer(d)).start()
        remote(r_ref.at[:, peer(d)], r_all.at[:, me], in_send.at[1], in_recv.at[1], plane=peer(d)).start()

    for l in range(LEVELS):
        for step in (1, -1):
            own_send(l, step).wait_recv()
            own_pass(l, step).start()

    def lines(l):
        for step in (1, -1):
            own_pass(l, step).wait_recv()
        for step in (1, -1):
            line_send(l, step).start()

    def passes(l):
        for step in (1, -1):
            line_send(l, step).wait_recv()
            line_pass(l, step).start()

    for l in (0, 1, 2, 3):
        lines(l)
    for l in (0, 1):
        passes(l)
    for l in (4, 5):
        lines(l)
    for l in (2, 3):
        passes(l)
    for l in (6, 7):
        lines(l)
    keep_c.wait()
    keep_r.wait()
    others = c_all.at[pl.ds(0, PEERS)]
    pltpu.make_async_copy(others, others, in_recv.at[0]).wait()
    others = r_all.at[:, pl.ds(0, PEERS)]
    pltpu.make_async_copy(others, others, in_recv.at[1]).wait()
    for i in range(ROWS):
        for l in range(LEVELS):
            right[l, i] = r_all[l, i].astype(jnp.float32)
            couple[l, i] = jnp.broadcast_to(c_all[i, l:l + 1], couple.shape[2:])
    for l in (4, 5, 6, 7):
        passes(l)

    tile = r_all.shape[2:]

    def pair(l, i, field):
        zero = jnp.zeros(tile, jnp.float32)
        before, here, there, after = [field(j) if 0 <= j < ROWS else zero for j in range(i - 1, i + 3)]
        left, right_ = wall.at[l, i // SIDE, i % SIDE], wall.at[l, (i + 1) // SIDE, (i + 1) % SIDE]
        centre = jnp.dot(
            jnp.concatenate([here, there], axis=1).astype(jnp.bfloat16),
            jnp.concatenate([left[BS:], right_[:2 * BS]], axis=1),
            preferred_element_type=jnp.float32)
        outer = jnp.concatenate(
            [jnp.concatenate([before, zero], axis=0), jnp.concatenate([zero, after], axis=0)], axis=1)
        outer = jnp.dot(
            outer.astype(jnp.bfloat16), jnp.concatenate([left[:BS], right_[2 * BS:]], axis=0),
            preferred_element_type=jnp.float32)
        half_ = tile[0]
        return centre[:, :BS] + outer[:half_], centre[:, BS:] + outer[half_:]

    def alive(l):
        return jnp.full(tile, live, jnp.int32) > l

    def chunk(ref, part):
        return ref.at[pl.ds(CHUNK * part, CHUNK)]

    def down_copy(part, where):
        return remote(chunk(down_out, part), chunk(down_in, part), hop_send.at[0, part], hop_recv.at[0, part], layer=where)

    def up_copy(part, where):
        return remote(chunk(up_out, part), chunk(up_in, part), hop_send.at[1, part], hop_recv.at[1, part], layer=where)

    def arrivals(copy, where, i):
        if i == 0:
            copy(0, where).wait_recv()
        part = (i + 2) // CHUNK
        if (i + 2) % CHUNK == 0 and part < ROWS // CHUNK:
            copy(part, where).wait_recv()

    def arrived(l):
        for step in (1, -1):
            line_pass(l, step).wait_recv()

    def down(start):
        now = {}

        def operand(l, i):
            if l > 0:
                return right[l, i] + couple[l, i] * now[l - 1, i]
            if start:
                return right[l, i]
            return right[l, i] + couple[l, i] * down_in[i].astype(jnp.float32)

        for l in range(LEVELS):
            if start:
                arrived(l)
            keep = alive(l)
            made = {}

            def field(i):
                if i not in made:
                    made[i] = operand(l, i)
                return made[i]

            for i in range(0, ROWS, 2):
                if l == 0 and not start:
                    arrivals(down_copy, s - 1, i)
                for j, value in zip((i, i + 1), pair(l, i, field)):
                    vals[l, j] = value
                    if l > 0:
                        value = jnp.where(keep, value, now[l - 1, j])
                    now[l, j] = value
                if l == LEVELS - 1:
                    for j in (i, i + 1):
                        down_out[j] = now[l, j].astype(jnp.bfloat16)
                    if (i + 2) % CHUNK == 0:
                        if start:
                            down_copy(i // CHUNK, s + 1).start()
                        else:
                            @pl.when(jnp.logical_not(last))
                            def _(part=i // CHUNK):
                                down_copy(part, s + 1).start()

    def out_copy(d, low, high):
        part = pl.ds(low, high - low)
        return remote(o_all.at[part, peer(d)], o_ref.at[part, me], out_send, out_recv, plane=peer(d))

    def out_sends(low, high):
        for d in range(1, ROWS):
            out_copy(d, low, high).start()

    def up(start, end):
        now = {}

        def field_at(l, i):
            return now[l + 1, i] if l < LEVELS - 1 else up_in[i].astype(jnp.float32)

        for l in reversed(range(LEVELS)):
            keep = alive(l)
            top = l == LEVELS - 1
            for i in range(0, ROWS, 2):
                if start and top:
                    sums = (0.0, 0.0)
                else:
                    if top:
                        arrivals(up_copy, s + 1, i)
                    sums = pair(l, i, lambda j: field_at(l, j))
                for j, total in zip((i, i + 1), sums):
                    answer = vals[l, j] + total
                    o_all[l, j] = jnp.where(keep, answer, 0.0).astype(jnp.bfloat16)
                    if l > 0 or not end:
                        behind = jnp.zeros(tile, jnp.float32) if start and top else field_at(l, j)
                        now[l, j] = jnp.where(keep, couple[l, j] * answer, behind)
                if l == 0 and not end:
                    for j in (i, i + 1):
                        up_out[j] = now[l, j].astype(jnp.bfloat16)
                    if (i + 2) % CHUNK == 0:
                        up_copy(i // CHUNK, s - 1).start()
            if end and l == 4:
                out_sends(4, 8)
            if end and l == 1:
                out_sends(1, 4)
        if end:
            out_sends(0, 1)
        else:
            out_sends(0, LEVELS)

    @pl.when(first)
    def _():
        down(True)

    @pl.when(jnp.logical_not(first))
    def _():
        for l in range(LEVELS):
            arrived(l)
        down(False)

    @pl.when(last)
    def _():
        up(True, False)

    @pl.when(jnp.logical_and(jnp.logical_not(first), jnp.logical_not(last)))
    def _():
        up(False, False)

    @pl.when(first)
    def _():
        up(False, True)

    o_ref[:, me] = o_all[:, me]

    for l in range(LEVELS):
        for step in (1, -1):
            for send in (own_send, own_pass, line_send, line_pass):
                send(l, step).wait_send()
    others = c_all.at[pl.ds(0, PEERS)]
    pltpu.make_async_copy(others, others, in_send.at[0]).wait()
    others = r_all.at[:, pl.ds(0, PEERS)]
    pltpu.make_async_copy(others, others, in_send.at[1]).wait()

    @pl.when(jnp.logical_not(last))
    def _():
        for part in range(ROWS // CHUNK):
            down_copy(part, s + 1).wait_send()

    @pl.when(jnp.logical_not(first))
    def _():
        for part in range(ROWS // CHUNK):
            up_copy(part, s - 1).wait_send()

    others = o_all.at[:, pl.ds(0, PEERS)]
    pltpu.make_async_copy(others, others, out_send).wait()
    others = o_ref.at[:, pl.ds(0, PEERS)]
    pltpu.make_async_copy(others, others, out_recv).wait()


def sweep(lengths, index, right, coupling, blocks):
    levels, _, cols, _ = right.shape
    per_row = blocks.shape[2]
    vmem = pl.BlockSpec(memory_space=pltpu.VMEM)
    smem = pl.BlockSpec(memory_space=pltpu.SMEM)
    hbm = pl.BlockSpec(memory_space=pl.ANY)
    field = pltpu.VMEM((ROWS, cols, BS), jnp.bfloat16)
    stack = pltpu.VMEM((levels, ROWS, cols, BS), jnp.bfloat16)
    wide = pltpu.VMEM((levels, ROWS, cols, BS), jnp.float32)
    dma = pltpu.SemaphoreType.DMA
    return pl.pallas_call(
        sweep_kernel,
        in_specs=[smem, smem, hbm, hbm, hbm],
        out_specs=vmem,
        out_shape=jax.ShapeDtypeStruct(right.shape, jnp.bfloat16),
        scratch_shapes=[
            pltpu.VMEM((levels, per_row, BS, BS), jnp.bfloat16),
            pltpu.VMEM((levels, SIDE, SIDE, 3 * BS, BS), jnp.bfloat16),
            stack,
            pltpu.VMEM((ROWS, levels, BS), jnp.float32),
            stack,
            wide, wide, wide,
            field, field, field, field,
            dma((levels,)), dma((2,)), dma((levels, 8)), dma((levels, 8)),
            dma((2,)), dma((2,)), dma, dma, dma((2, ROWS // CHUNK)), dma((2, ROWS // CHUNK)),
            pltpu.SemaphoreType.REGULAR((3,)),
        ],
        compiler_params=pltpu.CompilerParams(
            collective_id=0, has_side_effects=True, vmem_limit_bytes=60 * 1024 * 1024),
        name="sweep",
    )(lengths, index, right, coupling, blocks)


def on_device(right_sides, coupling, blocks, block_index, section_lengths):
    levels, columns, width = right_sides.shape
    right = right_sides.reshape(levels, ROWS, columns // ROWS, width)
    out = sweep(section_lengths, block_index, right, coupling, blocks)
    return out.reshape(levels, columns, width)


def solution(mesh):
    return jax.shard_map(
        on_device,
        mesh=mesh,
        in_specs=(
            P("layer", None, "plane"),
            P("layer", "plane"),
            P("layer", "plane", None, None, None),
            P("layer", "plane", None),
            P("layer"),
        ),
        out_specs=P("layer", None, "plane"),
        check_vma=False,
    )
```

```python
import jax
import jax.numpy as jnp
from jax import lax
from jax.experimental import pallas as pl
from jax.experimental.pallas import tpu as pltpu
from jax.sharding import PartitionSpec as P

MESH = pl.DeviceIdType.MESH
BS = 128
SIDE = 4
LEVELS = 8
ROWS = SIDE * SIDE
PEERS = ROWS - 1
CHUNK = 16


def sweep_kernel(len_ref, idx_ref, r_ref, c_ref, blocks_ref, o_ref,
                 raw, wall, r_own, r_all, c_own, c_all, o_all, right, couple, vals, down_in, up_in, down_out, up_out,
                 raw_sem, stage_sem, g_send, g_recv, in_send, in_recv, out_send, out_recv, hop_send, hop_recv, rounds):
    sections = lax.axis_size("layer")
    s, me = lax.axis_index("layer"), lax.axis_index("plane")
    x, y = me // SIDE, lax.rem(me, SIDE)
    live = len_ref[0]
    first, last = s == 0, s == sections - 1
    per_row = raw.shape[1]

    stage_c = pltpu.make_async_copy(c_ref, c_own, stage_sem.at[LEVELS])
    stage_r = [pltpu.make_async_copy(r_ref.at[l], r_own.at[:, l], stage_sem.at[l]) for l in range(LEVELS)]
    loads = [pltpu.make_async_copy(blocks_ref.at[l, 0], raw.at[l], raw_sem.at[l]) for l in range(LEVELS)]
    for load in loads[:2] + [stage_c] + stage_r + loads[2:]:
        load.start()

    def peer(d):
        return lax.rem(me + d, ROWS)

    barrier = pltpu.get_barrier_semaphore()
    for near in (lax.rem(s + 1, sections), lax.rem(s + sections - 1, sections)):
        pl.semaphore_signal(barrier, inc=1, device_id={"layer": near}, device_id_type=MESH)
    def at(dx, dy):
        return lax.rem(x + dx + SIDE, SIDE) * SIDE + lax.rem(y + dy + SIDE, SIDE)

    beside = [at(1, 0), at(-1, 0), at(0, 1), at(0, -1)]
    for near in beside:
        pl.semaphore_signal(barrier, inc=1, device_id={"plane": near}, device_id_type=MESH)

    def spread(turn):
        for near in beside:
            pl.semaphore_signal(rounds.at[turn], inc=1, device_id={"plane": near}, device_id_type=MESH)
        pl.semaphore_wait(rounds.at[turn], len(beside))

    def collapse(l):
        loads[l].wait()
        picks = [[(idx_ref[l, 0, t] == b).astype(jnp.float32) for b in range(3)] for t in range(per_row)]
        for b in range(3):
            total = raw[l, 0].astype(jnp.float32) * picks[0][b]
            for t in range(1, per_row):
                total += raw[l, t].astype(jnp.float32) * picks[t][b]
            wall[l, x, y, b * BS:(b + 1) * BS, :] = total.T.astype(jnp.bfloat16)

    def remote(src, dst, send, recv, **where):
        return pltpu.make_async_remote_copy(
            src_ref=src, dst_ref=dst, send_sem=send, recv_sem=recv, device_id=where, device_id_type=MESH)

    def near(axis, step):
        return at(step, 0) if axis == 0 else at(0, step)

    def shift(value, step):
        return lax.rem(value + step + SIDE, SIDE)

    half = 3 * BS // 2

    def own_send(l, step):
        slot = 0 if step == 1 else 1
        ref = wall.at[l, x, y]
        return remote(ref, ref, g_send.at[l, slot], g_recv.at[l, slot], plane=near(l % 2 == 0, step))

    def own_pass(l, step):
        slot = 2 if step == 1 else 3
        sx, sy = (x, shift(y, -step)) if l % 2 == 0 else (shift(x, -step), y)
        ref = wall.at[l, sx, sy, pl.ds(0 if step == 1 else half, half)]
        return remote(ref, ref, g_send.at[l, slot], g_recv.at[l, slot], plane=near(l % 2 == 0, step))

    def line_send(l, step):
        slot = 4 if step == 1 else 5
        ref = wall.at[l, x] if l % 2 == 0 else wall.at[l, :, y]
        return remote(ref, ref, g_send.at[l, slot], g_recv.at[l, slot], plane=near(l % 2 == 1, step))

    def line_pass(l, step):
        slot = 6 if step == 1 else 7
        part = pl.ds(0 if step == 1 else 2, 2)
        ref = wall.at[l, shift(x, -step), part] if l % 2 == 0 else wall.at[l, part, shift(y, -step)]
        return remote(ref, ref, g_send.at[l, slot], g_recv.at[l, slot], plane=near(l % 2 == 1, step))

    collapse(0)
    pl.semaphore_wait(barrier, 2 + len(beside))
    for l in range(LEVELS):
        if l > 0:
            collapse(l)
        for step in (1, -1):
            own_send(l, step).start()
    for l in range(LEVELS):
        if l in (0, 2, 4):
            spread(l // 2)
        for step in (1, -1):
            own_send(l, step).wait_recv()
            own_pass(l, step).start()

    def lines(l):
        for step in (1, -1):
            own_pass(l, step).wait_recv()
        for step in (1, -1):
            line_send(l, step).start()

    def passes(l):
        for step in (1, -1):
            line_send(l, step).wait_recv()
            line_pass(l, step).start()

    for l in (0, 1, 2, 3):
        lines(l)
    stage_c.wait()
    for copy in stage_r:
        copy.wait()
    for d in range(1, ROWS):
        remote(c_own, c_all.at[me], in_send.at[0], in_recv.at[0], plane=peer(d)).start()
        remote(r_own.at[peer(d)], r_all.at[me], in_send.at[1], in_recv.at[1], plane=peer(d)).start()
    c_all[me] = c_own[...]
    r_all[me] = r_own[me]
    for l in (0, 1):
        passes(l)
    for l in (4, 5):
        lines(l)
    for l in (2, 3):
        passes(l)
    for l in (6, 7):
        lines(l)
    others = c_all.at[pl.ds(0, PEERS)]
    pltpu.make_async_copy(others, others, in_recv.at[0]).wait()
    others = r_all.at[pl.ds(0, PEERS)]
    pltpu.make_async_copy(others, others, in_recv.at[1]).wait()
    for i in range(ROWS):
        for l in range(LEVELS):
            right[l, i] = r_all[i, l].astype(jnp.float32)
            couple[l, i] = jnp.broadcast_to(c_all[i, l:l + 1], couple.shape[2:])
    for l in (4, 5, 6, 7):
        passes(l)

    tile = r_all.shape[2:]

    def pair(l, i, field):
        zero = jnp.zeros(tile, jnp.float32)
        before, here, there, after = [field(j) if 0 <= j < ROWS else zero for j in range(i - 1, i + 3)]
        left, right_ = wall.at[l, i // SIDE, i % SIDE], wall.at[l, (i + 1) // SIDE, (i + 1) % SIDE]
        centre = jnp.dot(
            jnp.concatenate([here, there], axis=1).astype(jnp.bfloat16),
            jnp.concatenate([left[BS:], right_[:2 * BS]], axis=1),
            preferred_element_type=jnp.float32)
        outer = jnp.concatenate(
            [jnp.concatenate([before, zero], axis=0), jnp.concatenate([zero, after], axis=0)], axis=1)
        outer = jnp.dot(
            outer.astype(jnp.bfloat16), jnp.concatenate([left[:BS], right_[2 * BS:]], axis=0),
            preferred_element_type=jnp.float32)
        half_ = tile[0]
        return centre[:, :BS] + outer[:half_], centre[:, BS:] + outer[half_:]

    def alive(l):
        return jnp.full(tile, live, jnp.int32) > l

    def chunk(ref, part):
        return ref.at[pl.ds(CHUNK * part, CHUNK)]

    def down_copy(part, where):
        return remote(chunk(down_out, part), chunk(down_in, part), hop_send.at[0, part], hop_recv.at[0, part], layer=where)

    def up_copy(part, where):
        return remote(chunk(up_out, part), chunk(up_in, part), hop_send.at[1, part], hop_recv.at[1, part], layer=where)

    def arrivals(copy, where, i):
        if i == 0:
            copy(0, where).wait_recv()
        part = (i + 2) // CHUNK
        if (i + 2) % CHUNK == 0 and part < ROWS // CHUNK:
            copy(part, where).wait_recv()

    def arrived(l):
        for step in (1, -1):
            line_pass(l, step).wait_recv()

    def down(start):
        now = {}

        def operand(l, i):
            if l > 0:
                return right[l, i] + couple[l, i] * now[l - 1, i]
            if start:
                return right[l, i]
            return right[l, i] + couple[l, i] * down_in[i].astype(jnp.float32)

        for l in range(LEVELS):
            if start:
                arrived(l)
            keep = alive(l)
            made = {}

            def field(i):
                if i not in made:
                    made[i] = operand(l, i)
                return made[i]

            for i in range(0, ROWS, 2):
                if l == 0 and not start:
                    arrivals(down_copy, s - 1, i)
                for j, value in zip((i, i + 1), pair(l, i, field)):
                    vals[l, j] = value
                    if l > 0:
                        value = jnp.where(keep, value, now[l - 1, j])
                    now[l, j] = value
                if l == LEVELS - 1:
                    for j in (i, i + 1):
                        down_out[j] = now[l, j].astype(jnp.bfloat16)
                    if (i + 2) % CHUNK == 0:
                        if start:
                            down_copy(i // CHUNK, s + 1).start()
                        else:
                            @pl.when(jnp.logical_not(last))
                            def _(part=i // CHUNK):
                                down_copy(part, s + 1).start()

    def out_copy(d, low, high):
        part = pl.ds(low, high - low)
        return remote(o_all.at[part, peer(d)], o_ref.at[part, me], out_send, out_recv, plane=peer(d))

    def out_sends(low, high):
        for d in range(1, ROWS):
            out_copy(d, low, high).start()

    def up(start, end):
        now = {}

        def field_at(l, i):
            return now[l + 1, i] if l < LEVELS - 1 else up_in[i].astype(jnp.float32)

        for l in reversed(range(LEVELS)):
            keep = alive(l)
            top = l == LEVELS - 1
            for i in range(0, ROWS, 2):
                if start and top:
                    sums = (0.0, 0.0)
                else:
                    if top:
                        arrivals(up_copy, s + 1, i)
                    sums = pair(l, i, lambda j: field_at(l, j))
                for j, total in zip((i, i + 1), sums):
                    answer = vals[l, j] + total
                    o_all[l, j] = jnp.where(keep, answer, 0.0).astype(jnp.bfloat16)
                    if l > 0 or not end:
                        behind = jnp.zeros(tile, jnp.float32) if start and top else field_at(l, j)
                        now[l, j] = jnp.where(keep, couple[l, j] * answer, behind)
                if l == 0 and not end:
                    for j in (i, i + 1):
                        up_out[j] = now[l, j].astype(jnp.bfloat16)
                    if (i + 2) % CHUNK == 0:
                        up_copy(i // CHUNK, s - 1).start()
            if end and l == 4:
                out_sends(4, 8)
            if end and l == 1:
                out_sends(1, 4)
        if end:
            out_sends(0, 1)
        else:
            out_sends(0, LEVELS)

    @pl.when(first)
    def _():
        down(True)

    @pl.when(jnp.logical_not(first))
    def _():
        for l in range(LEVELS):
            arrived(l)
        down(False)

    @pl.when(last)
    def _():
        up(True, False)

    @pl.when(jnp.logical_and(jnp.logical_not(first), jnp.logical_not(last)))
    def _():
        up(False, False)

    @pl.when(first)
    def _():
        up(False, True)

    o_ref[:, me] = o_all[:, me]

    for l in range(LEVELS):
        for step in (1, -1):
            for send in (own_send, own_pass, line_send, line_pass):
                send(l, step).wait_send()
    others = c_all.at[pl.ds(0, PEERS)]
    pltpu.make_async_copy(others, others, in_send.at[0]).wait()
    others = r_all.at[pl.ds(0, PEERS)]
    pltpu.make_async_copy(others, others, in_send.at[1]).wait()

    @pl.when(jnp.logical_not(last))
    def _():
        for part in range(ROWS // CHUNK):
            down_copy(part, s + 1).wait_send()

    @pl.when(jnp.logical_not(first))
    def _():
        for part in range(ROWS // CHUNK):
            up_copy(part, s - 1).wait_send()

    others = o_all.at[:, pl.ds(0, PEERS)]
    pltpu.make_async_copy(others, others, out_send).wait()
    others = o_ref.at[:, pl.ds(0, PEERS)]
    pltpu.make_async_copy(others, others, out_recv).wait()


def sweep(lengths, index, right, coupling, blocks):
    levels, _, cols, _ = right.shape
    per_row = blocks.shape[2]
    vmem = pl.BlockSpec(memory_space=pltpu.VMEM)
    smem = pl.BlockSpec(memory_space=pltpu.SMEM)
    hbm = pl.BlockSpec(memory_space=pl.ANY)
    field = pltpu.VMEM((ROWS, cols, BS), jnp.bfloat16)
    stack = pltpu.VMEM((levels, ROWS, cols, BS), jnp.bfloat16)
    inputs = pltpu.VMEM((ROWS, levels, cols, BS), jnp.bfloat16)
    wide = pltpu.VMEM((levels, ROWS, cols, BS), jnp.float32)
    dma = pltpu.SemaphoreType.DMA
    return pl.pallas_call(
        sweep_kernel,
        in_specs=[smem, smem, hbm, hbm, hbm],
        out_specs=vmem,
        out_shape=jax.ShapeDtypeStruct(right.shape, jnp.bfloat16),
        scratch_shapes=[
            pltpu.VMEM((levels, per_row, BS, BS), jnp.bfloat16),
            pltpu.VMEM((levels, SIDE, SIDE, 3 * BS, BS), jnp.bfloat16),
            inputs, inputs,
            pltpu.VMEM((levels, BS), jnp.float32),
            pltpu.VMEM((ROWS, levels, BS), jnp.float32),
            stack,
            wide, wide, wide,
            field, field, field, field,
            dma((levels,)), dma((levels + 1,)), dma((levels, 8)), dma((levels, 8)),
            dma((2,)), dma((2,)), dma, dma, dma((2, ROWS // CHUNK)), dma((2, ROWS // CHUNK)),
            pltpu.SemaphoreType.REGULAR((3,)),
        ],
        compiler_params=pltpu.CompilerParams(
            collective_id=0, has_side_effects=True, vmem_limit_bytes=57 * 1024 * 1024),
        name="sweep",
    )(lengths, index, right, coupling, blocks)


def on_device(right_sides, coupling, blocks, block_index, section_lengths):
    levels, columns, width = right_sides.shape
    right = right_sides.reshape(levels, ROWS, columns // ROWS, width)
    out = sweep(section_lengths, block_index, right, coupling, blocks)
    return out.reshape(levels, columns, width)


def solution(mesh):
    return jax.shard_map(
        on_device,
        mesh=mesh,
        in_specs=(
            P("layer", None, "plane"),
            P("layer", "plane"),
            P("layer", "plane", None, None, None),
            P("layer", "plane", None),
            P("layer"),
        ),
        out_specs=P("layer", None, "plane"),
        check_vma=False,
    )
```

```python
import jax
import jax.numpy as jnp
from jax import lax
from jax.experimental import pallas as pl
from jax.experimental.pallas import tpu as pltpu
from jax.sharding import PartitionSpec as P

MESH = pl.DeviceIdType.MESH
BS = 128
SIDE = 4
LEVELS = 8
ROWS = SIDE * SIDE
PEERS = ROWS - 1
CHUNK = 16


def sweep_kernel(len_ref, idx_ref, r_ref, c_ref, blocks_ref, o_ref,
                 raw, wall, wall2, r_own, r_all, r2_all, c_own, c_all, c2_all, len_own, len2, o_all, right, couple, vals, down_in, up_in, down_out, up_out,
                 raw_sem, stage_sem, g_send, g_recv, in_send, in_recv, out_send, out_recv, hop_send, hop_recv, rounds, keep_sem, f_send, f_recv, e_send, e_recv, out_send2):
    sections = lax.axis_size("layer")
    s, me = lax.axis_index("layer"), lax.axis_index("plane")
    x, y = me // SIDE, lax.rem(me, SIDE)
    live = len_ref[0]
    worker = lax.rem(s, 2) == 0
    helper = lax.rem(s, 2) == 1
    first, last = s == 0, s == sections - 2
    per_row = raw.shape[1]

    stage_c = pltpu.make_async_copy(c_ref, c_own, stage_sem.at[LEVELS])
    stage_r = [pltpu.make_async_copy(r_ref.at[l], r_own.at[:, l], stage_sem.at[l]) for l in range(LEVELS)]
    loads = [pltpu.make_async_copy(blocks_ref.at[l, 0], raw.at[l], raw_sem.at[l]) for l in range(LEVELS)]
    for load in loads[:2] + [stage_c] + stage_r + loads[2:]:
        load.start()

    def peer(d):
        return lax.rem(me + d, ROWS)

    barrier = pltpu.get_barrier_semaphore()
    for near in [lax.rem(s + step + sections, sections) for step in (1, -1, 2, -2)]:
        pl.semaphore_signal(barrier, inc=1, device_id={"layer": near}, device_id_type=MESH)
    def at(dx, dy):
        return lax.rem(x + dx + SIDE, SIDE) * SIDE + lax.rem(y + dy + SIDE, SIDE)

    beside = [at(1, 0), at(-1, 0), at(0, 1), at(0, -1)]
    for near in beside:
        pl.semaphore_signal(barrier, inc=1, device_id={"plane": near}, device_id_type=MESH)

    def spread(turn):
        for near in beside:
            pl.semaphore_signal(rounds.at[turn], inc=1, device_id={"plane": near}, device_id_type=MESH)
        pl.semaphore_wait(rounds.at[turn], len(beside))

    def collapse(l):
        loads[l].wait()
        picks = [[(idx_ref[l, 0, t] == b).astype(jnp.float32) for b in range(3)] for t in range(per_row)]
        for b in range(3):
            total = raw[l, 0].astype(jnp.float32) * picks[0][b]
            for t in range(1, per_row):
                total += raw[l, t].astype(jnp.float32) * picks[t][b]
            wall[l, x, y, b * BS:(b + 1) * BS, :] = total.T.astype(jnp.bfloat16)

    def remote(src, dst, send, recv, **where):
        return pltpu.make_async_remote_copy(
            src_ref=src, dst_ref=dst, send_sem=send, recv_sem=recv, device_id=where, device_id_type=MESH)

    def near(axis, step):
        return at(step, 0) if axis == 0 else at(0, step)

    def shift(value, step):
        return lax.rem(value + step + SIDE, SIDE)

    half = 3 * BS // 2

    def own_send(l, step):
        slot = 0 if step == 1 else 1
        ref = wall.at[l, x, y]
        return remote(ref, ref, g_send.at[l, slot], g_recv.at[l, slot], plane=near(l % 2 == 0, step))

    def own_pass(l, step):
        slot = 2 if step == 1 else 3
        sx, sy = (x, shift(y, -step)) if l % 2 == 0 else (shift(x, -step), y)
        ref = wall.at[l, sx, sy, pl.ds(0, half) if step == 1 else pl.ds(half, 3 * BS - half)]
        return remote(ref, ref, g_send.at[l, slot], g_recv.at[l, slot], plane=near(l % 2 == 0, step))

    def line_send(l, step):
        slot = 4 if step == 1 else 5
        ref = wall.at[l, x] if l % 2 == 0 else wall.at[l, :, y]
        return remote(ref, ref, g_send.at[l, slot], g_recv.at[l, slot], plane=near(l % 2 == 1, step))

    def line_pass(l, step):
        slot = 6 if step == 1 else 7
        part = pl.ds(0 if step == 1 else 2, 2)
        ref = wall.at[l, shift(x, -step), part] if l % 2 == 0 else wall.at[l, part, shift(y, -step)]
        return remote(ref, ref, g_send.at[l, slot], g_recv.at[l, slot], plane=near(l % 2 == 1, step))

    collapse(0)
    pl.semaphore_wait(barrier, 4 + len(beside))
    for l in range(LEVELS):
        if l > 0:
            collapse(l)
        for step in (1, -1):
            own_send(l, step).start()
    for l in range(LEVELS):
        if l in (0, 2, 4):
            spread(l // 2)
        for step in (1, -1):
            own_send(l, step).wait_recv()
            own_pass(l, step).start()

    def hand(l, k):
        if k < 3:
            step = (0, -1, 1)[k]
            at_ = (l, shift(x, step)) if l % 2 == 0 else (l, slice(None), shift(y, step))
        else:
            part = pl.ds(0 if k == 3 else 2, 2)
            at_ = (l, shift(x, 2), part) if l % 2 == 0 else (l, part, shift(y, 2))
        return remote(wall.at[at_], wall2.at[at_], f_send.at[l, k], f_recv.at[l, k], layer=s - 1)

    def hand_over(l, k):
        @pl.when(helper)
        def _():
            hand(l, k).start()

    def lines(l):
        for step in (1, -1):
            own_pass(l, step).wait_recv()
        hand_over(l, 0)
        for step in (1, -1):
            line_send(l, step).start()

    def passes(l):
        for step in (1, -1):
            line_send(l, step).wait_recv()
            line_pass(l, step).start()
            hand_over(l, 1 if step == 1 else 2)

    for l in (0, 1, 2, 3):
        lines(l)
    stage_c.wait()
    for copy in stage_r:
        copy.wait()
    for d in range(1, ROWS):
        remote(c_own, c_all.at[me], in_send.at[0], in_recv.at[0], plane=peer(d)).start()
        remote(r_own.at[peer(d)], r_all.at[me], in_send.at[1], in_recv.at[1], plane=peer(d)).start()
    c_all[me] = c_own[...]
    r_all[me] = r_own[me]
    for l in (0, 1):
        passes(l)
    for l in (4, 5):
        lines(l)
    for l in (2, 3):
        passes(l)
    for l in (6, 7):
        lines(l)
    others = c_all.at[pl.ds(0, PEERS)]
    pltpu.make_async_copy(others, others, in_recv.at[0]).wait()
    others = r_all.at[pl.ds(0, PEERS)]
    pltpu.make_async_copy(others, others, in_recv.at[1]).wait()
    def extras():
        return [remote(src, dst, e_send.at[k], e_recv.at[k], layer=s - 1)
                for k, (src, dst) in enumerate(((r_all, r2_all), (c_all, c2_all), (len_own, len2)))]

    @pl.when(helper)
    def _():
        len_own[...] = jnp.full(len_own.shape, live, jnp.int32)
        for copy in extras():
            copy.start()

    for l in (4, 5):
        passes(l)

    @pl.when(worker)
    def _():
        for copy in extras():
            copy.wait_recv()
        for i in range(ROWS):
            for l in range(LEVELS):
                right[l, i] = r_all[i, l].astype(jnp.float32)
                couple[l, i] = jnp.broadcast_to(c_all[i, l:l + 1], couple.shape[2:])
                right[LEVELS + l, i] = r2_all[i, l].astype(jnp.float32)
                couple[LEVELS + l, i] = jnp.broadcast_to(c2_all[i, l:l + 1], couple.shape[2:])

    for l in (6, 7):
        passes(l)

    tile = r_all.shape[2:]

    def pair(l, i, field):
        zero = jnp.zeros(tile, jnp.float32)
        before, here, there, after = [field(j) if 0 <= j < ROWS else zero for j in range(i - 1, i + 3)]
        store, l = (wall, l) if l < LEVELS else (wall2, l - LEVELS)
        left, right_ = store.at[l, i // SIDE, i % SIDE], store.at[l, (i + 1) // SIDE, (i + 1) % SIDE]
        centre = jnp.dot(
            jnp.concatenate([here, there], axis=1).astype(jnp.bfloat16),
            jnp.concatenate([left[BS:], right_[:2 * BS]], axis=1),
            preferred_element_type=jnp.float32)
        outer = jnp.concatenate(
            [jnp.concatenate([before, zero], axis=0), jnp.concatenate([zero, after], axis=0)], axis=1)
        outer = jnp.dot(
            outer.astype(jnp.bfloat16), jnp.concatenate([left[:BS], right_[2 * BS:]], axis=0),
            preferred_element_type=jnp.float32)
        half_ = tile[0]
        return centre[:, :BS] + outer[:half_], centre[:, BS:] + outer[half_:]

    def alive(l):
        return jnp.full(tile, live, jnp.int32) > l if l < LEVELS else len2[...] > l - LEVELS

    def chunk(ref, part):
        return ref.at[pl.ds(CHUNK * part, CHUNK)]

    def down_copy(part, where):
        return remote(chunk(down_out, part), chunk(down_in, part), hop_send.at[0, part], hop_recv.at[0, part], layer=where)

    def up_copy(part, where):
        return remote(chunk(up_out, part), chunk(up_in, part), hop_send.at[1, part], hop_recv.at[1, part], layer=where)

    def arrivals(copy, where, i):
        if i == 0:
            copy(0, where).wait_recv()
        part = (i + 2) // CHUNK
        if (i + 2) % CHUNK == 0 and part < ROWS // CHUNK:
            copy(part, where).wait_recv()

    def arrived(l):
        if l < LEVELS:
            for step in (1, -1):
                line_pass(l, step).wait_recv()
        else:
            for k in range(5):
                hand(l - LEVELS, k).wait_recv()

    def down(start):
        now = {}

        def operand(l, i):
            if l > 0:
                return right[l, i] + couple[l, i] * now[l - 1, i]
            if start:
                return right[l, i]
            return right[l, i] + couple[l, i] * down_in[i].astype(jnp.float32)

        for l in range(2 * LEVELS):
            if start:
                arrived(l)
            keep = alive(l)
            made = {}

            def field(i):
                if i not in made:
                    made[i] = operand(l, i)
                return made[i]

            for i in range(0, ROWS, 2):
                if l == 0 and not start:
                    arrivals(down_copy, s - 2, i)
                for j, value in zip((i, i + 1), pair(l, i, field)):
                    vals[l, j] = value
                    if l > 0:
                        value = jnp.where(keep, value, now[l - 1, j])
                    now[l, j] = value
                if l == 2 * LEVELS - 1:
                    for j in (i, i + 1):
                        down_out[j] = now[l, j].astype(jnp.bfloat16)
                    if (i + 2) % CHUNK == 0:
                        if start:
                            down_copy(i // CHUNK, s + 2).start()
                        else:
                            @pl.when(jnp.logical_not(last))
                            def _(part=i // CHUNK):
                                down_copy(part, s + 2).start()

    def out_copy(d, low, high):
        part = pl.ds(low, high - low)
        return remote(o_all.at[part, peer(d)], o_ref.at[part, me], out_send, out_recv, plane=peer(d))

    def out_sends2():
        for d in range(ROWS):
            remote(o_all.at[pl.ds(LEVELS, LEVELS), peer(d)], o_ref.at[:, me], out_send2, out_recv,
                   layer=s + 1, plane=peer(d)).start()

    def out_sends(low, high):
        for d in range(1, ROWS):
            out_copy(d, low, high).start()

    def up(start, end):
        now = {}

        def field_at(l, i):
            return now[l + 1, i] if l < 2 * LEVELS - 1 else up_in[i].astype(jnp.float32)

        for l in reversed(range(2 * LEVELS)):
            keep = alive(l)
            top = l == 2 * LEVELS - 1
            for i in range(0, ROWS, 2):
                if start and top:
                    sums = (0.0, 0.0)
                else:
                    if top:
                        arrivals(up_copy, s + 2, i)
                    sums = pair(l, i, lambda j: field_at(l, j))
                for j, total in zip((i, i + 1), sums):
                    answer = vals[l, j] + total
                    o_all[l, j] = jnp.where(keep, answer, 0.0).astype(jnp.bfloat16)
                    if l > 0 or not end:
                        behind = jnp.zeros(tile, jnp.float32) if start and top else field_at(l, j)
                        now[l, j] = jnp.where(keep, couple[l, j] * answer, behind)
                if l == 0 and not end:
                    for j in (i, i + 1):
                        up_out[j] = now[l, j].astype(jnp.bfloat16)
                    if (i + 2) % CHUNK == 0:
                        up_copy(i // CHUNK, s - 2).start()
            if end and l == LEVELS:
                out_sends2()
            if end and l == 4:
                out_sends(4, 8)
            if end and l == 1:
                out_sends(1, 4)
        if end:
            out_sends(0, 1)
        else:
            out_sends2()
            out_sends(0, LEVELS)

    @pl.when(helper)
    def _():
        for l in range(LEVELS):
            for step in (1, -1):
                line_pass(l, step).wait_recv()
                hand(l, 3 if step == 1 else 4).start()

    @pl.when(first)
    def _():
        down(True)

    @pl.when(jnp.logical_and(worker, jnp.logical_not(first)))
    def _():
        for l in range(2 * LEVELS):
            arrived(l)
        down(False)

    @pl.when(last)
    def _():
        up(True, False)

    @pl.when(jnp.logical_and(worker, jnp.logical_and(jnp.logical_not(first), jnp.logical_not(last))))
    def _():
        up(False, False)

    @pl.when(first)
    def _():
        up(False, True)

    for l in range(LEVELS):
        for step in (1, -1):
            for send in (own_send, own_pass, line_send, line_pass):
                send(l, step).wait_send()
    others = c_all.at[pl.ds(0, PEERS)]
    pltpu.make_async_copy(others, others, in_send.at[0]).wait()
    others = r_all.at[pl.ds(0, PEERS)]
    pltpu.make_async_copy(others, others, in_send.at[1]).wait()

    @pl.when(jnp.logical_and(worker, jnp.logical_not(last)))
    def _():
        down_copy(0, s + 2).wait_send()

    @pl.when(jnp.logical_and(worker, jnp.logical_not(first)))
    def _():
        up_copy(0, s - 2).wait_send()

    @pl.when(worker)
    def _():
        keep = pltpu.make_async_copy(o_all.at[pl.ds(0, LEVELS), me], o_ref.at[:, me], keep_sem)
        keep.start()
        others = o_all.at[pl.ds(0, LEVELS), pl.ds(0, PEERS)]
        pltpu.make_async_copy(others, others, out_send).wait()
        others = o_all.at[pl.ds(LEVELS, LEVELS)]
        pltpu.make_async_copy(others, others, out_send2).wait()
        keep.wait()
        others = o_ref.at[:, pl.ds(0, PEERS)]
        pltpu.make_async_copy(others, others, out_recv).wait()

    @pl.when(helper)
    def _():
        for l in range(LEVELS):
            for k in range(5):
                hand(l, k).wait_send()
        for copy in extras():
            copy.wait_send()
        pltpu.make_async_copy(o_ref, o_ref, out_recv).wait()


def sweep(lengths, index, right, coupling, blocks):
    levels, _, cols, _ = right.shape
    per_row = blocks.shape[2]
    smem = pl.BlockSpec(memory_space=pltpu.SMEM)
    hbm = pl.BlockSpec(memory_space=pl.ANY)
    field = pltpu.VMEM((ROWS, cols, BS), jnp.bfloat16)
    stack = pltpu.VMEM((2 * levels, ROWS, cols, BS), jnp.bfloat16)
    inputs = pltpu.VMEM((ROWS, levels, cols, BS), jnp.bfloat16)
    wide = pltpu.VMEM((2 * levels, ROWS, cols, BS), jnp.float32)
    dma = pltpu.SemaphoreType.DMA
    return pl.pallas_call(
        sweep_kernel,
        in_specs=[smem, smem, hbm, hbm, hbm],
        out_specs=hbm,
        out_shape=jax.ShapeDtypeStruct(right.shape, jnp.bfloat16),
        scratch_shapes=[
            pltpu.VMEM((levels, per_row, BS, BS), jnp.bfloat16),
            pltpu.VMEM((levels, SIDE, SIDE, 3 * BS, BS), jnp.bfloat16),
            pltpu.VMEM((levels, SIDE, SIDE, 3 * BS, BS), jnp.bfloat16),
            inputs, inputs, inputs,
            pltpu.VMEM((levels, BS), jnp.float32),
            pltpu.VMEM((ROWS, levels, BS), jnp.float32),
            pltpu.VMEM((ROWS, levels, BS), jnp.float32),
            pltpu.VMEM((cols, BS), jnp.int32),
            pltpu.VMEM((cols, BS), jnp.int32),
            stack,
            wide, wide, wide,
            field, field, field, field,
            dma((levels,)), dma((levels + 1,)), dma((levels, 8)), dma((levels, 8)),
            dma((2,)), dma((2,)), dma, dma, dma((2, ROWS // CHUNK)), dma((2, ROWS // CHUNK)),
            pltpu.SemaphoreType.REGULAR((3,)), dma,
            dma((levels, 5)), dma((levels, 5)), dma((3,)), dma((3,)), dma,
        ],
        compiler_params=pltpu.CompilerParams(
            collective_id=0, has_side_effects=True, vmem_limit_bytes=57 * 1024 * 1024),
        name="sweep",
    )(lengths, index, right, coupling, blocks)


def on_device(right_sides, coupling, blocks, block_index, section_lengths):
    levels, columns, width = right_sides.shape
    right = right_sides.reshape(levels, ROWS, columns // ROWS, width)
    out = sweep(section_lengths, block_index, right, coupling, blocks)
    return out.reshape(levels, columns, width)


def solution(mesh):
    return jax.shard_map(
        on_device,
        mesh=mesh,
        in_specs=(
            P("layer", None, "plane"),
            P("layer", "plane"),
            P("layer", "plane", None, None, None),
            P("layer", "plane", None),
            P("layer"),
        ),
        out_specs=P("layer", None, "plane"),
        check_vma=False,
    )
```

```python
import jax
import jax.numpy as jnp
from jax import lax
from jax.experimental import pallas as pl
from jax.experimental.pallas import tpu as pltpu
from jax.sharding import PartitionSpec as P

MESH = pl.DeviceIdType.MESH
BS = 128
SIDE = 4
LEVELS = 8
ROWS = SIDE * SIDE
PEERS = ROWS - 1
CHUNK = 16


def sweep_kernel(len_ref, idx_ref, r_ref, c_ref, blocks_ref, o_ref,
                 raw, wall, wall2, r_own, r_all, r2_all, c_own, c_all, c2_all, len_own, len2, o_all, right, couple, vals, down_in, up_in, down_out, up_out,
                 raw_sem, stage_sem, g_send, g_recv, in_send, in_recv, out_send, out_recv, hop_send, hop_recv, rounds, keep_sem, f_send, f_recv, e_send, e_recv, out_send2):
    sections = lax.axis_size("layer")
    s, me = lax.axis_index("layer"), lax.axis_index("plane")
    x, y = me // SIDE, lax.rem(me, SIDE)
    live = len_ref[0]
    worker = lax.rem(s, 2) == 0
    helper = lax.rem(s, 2) == 1
    partner = s + 1 - 2 * lax.rem(s, 2)
    first, last = s == 0, s == sections - 2
    per_row = raw.shape[1]

    stage_c = pltpu.make_async_copy(c_ref, c_own, stage_sem.at[LEVELS])
    stage_r = [pltpu.make_async_copy(r_ref.at[l], r_own.at[:, l], stage_sem.at[l]) for l in range(LEVELS)]
    loads = [pltpu.make_async_copy(blocks_ref.at[l, 0], raw.at[l], raw_sem.at[l]) for l in range(LEVELS)]
    for load in loads[:2] + [stage_c] + stage_r + loads[2:]:
        load.start()

    def peer(d):
        return lax.rem(me + d, ROWS)

    barrier = pltpu.get_barrier_semaphore()
    for near in [lax.rem(s + step + sections, sections) for step in (1, -1, 2, -2)]:
        pl.semaphore_signal(barrier, inc=1, device_id={"layer": near}, device_id_type=MESH)
    def at(dx, dy):
        return lax.rem(x + dx + SIDE, SIDE) * SIDE + lax.rem(y + dy + SIDE, SIDE)

    beside = [at(1, 0), at(-1, 0), at(0, 1), at(0, -1)]
    for near in beside:
        pl.semaphore_signal(barrier, inc=1, device_id={"plane": near}, device_id_type=MESH)

    def spread(turn):
        for near in beside:
            pl.semaphore_signal(rounds.at[turn], inc=1, device_id={"plane": near}, device_id_type=MESH)
        pl.semaphore_wait(rounds.at[turn], len(beside))

    def collapse(l):
        loads[l].wait()
        picks = [[(idx_ref[l, 0, t] == b).astype(jnp.float32) for b in range(3)] for t in range(per_row)]
        for b in range(3):
            total = raw[l, 0].astype(jnp.float32) * picks[0][b]
            for t in range(1, per_row):
                total += raw[l, t].astype(jnp.float32) * picks[t][b]
            wall[l, x, y, b * BS:(b + 1) * BS, :] = total.T.astype(jnp.bfloat16)

    def remote(src, dst, send, recv, **where):
        return pltpu.make_async_remote_copy(
            src_ref=src, dst_ref=dst, send_sem=send, recv_sem=recv, device_id=where, device_id_type=MESH)

    def near(axis, step):
        return at(step, 0) if axis == 0 else at(0, step)

    def shift(value, step):
        return lax.rem(value + step + SIDE, SIDE)

    half = 3 * BS // 2

    def own_send(l, step):
        slot = 0 if step == 1 else 1
        ref = wall.at[l, x, y]
        return remote(ref, ref, g_send.at[l, slot], g_recv.at[l, slot], plane=near(l % 2 == 0, step))

    def own_pass(l, step):
        slot = 2 if step == 1 else 3
        sx, sy = (x, shift(y, -step)) if l % 2 == 0 else (shift(x, -step), y)
        ref = wall.at[l, sx, sy, pl.ds(0, half) if step == 1 else pl.ds(half, 3 * BS - half)]
        return remote(ref, ref, g_send.at[l, slot], g_recv.at[l, slot], plane=near(l % 2 == 0, step))

    def line_send(l, step):
        slot = 4 if step == 1 else 5
        ref = wall.at[l, x] if l % 2 == 0 else wall.at[l, :, y]
        return remote(ref, ref, g_send.at[l, slot], g_recv.at[l, slot], plane=near(l % 2 == 1, step))

    def line_pass(l, step):
        slot = 6 if step == 1 else 7
        part = pl.ds(0 if step == 1 else 2, 2)
        ref = wall.at[l, shift(x, -step), part] if l % 2 == 0 else wall.at[l, part, shift(y, -step)]
        return remote(ref, ref, g_send.at[l, slot], g_recv.at[l, slot], plane=near(l % 2 == 1, step))

    collapse(0)
    pl.semaphore_wait(barrier, 4 + len(beside))
    for l in range(LEVELS):
        if l > 0:
            collapse(l)
        for step in (1, -1):
            own_send(l, step).start()
    for l in range(LEVELS):
        if l in (0, 2, 4):
            spread(l // 2)
        for step in (1, -1):
            own_send(l, step).wait_recv()
            own_pass(l, step).start()

    def hand(l, k):
        if k < 3:
            step = (0, -1, 1)[k]
            at_ = (l, shift(x, step)) if l % 2 == 0 else (l, slice(None), shift(y, step))
        else:
            part = pl.ds(0 if k == 3 else 2, 2)
            at_ = (l, shift(x, 2), part) if l % 2 == 0 else (l, part, shift(y, 2))
        return remote(wall.at[at_], wall2.at[at_], f_send.at[l, k], f_recv.at[l, k], layer=partner)

    def hand_over(l, k):
        @pl.when(helper)
        def _():
            hand(l, k).start()

    def lines(l):
        for step in (1, -1):
            own_pass(l, step).wait_recv()
        hand_over(l, 0)
        for step in (1, -1):
            line_send(l, step).start()

    def passes(l):
        for step in (1, -1):
            line_send(l, step).wait_recv()
            line_pass(l, step).start()
            hand_over(l, 1 if step == 1 else 2)

    for l in (0, 1, 2, 3):
        lines(l)
    stage_c.wait()
    for copy in stage_r:
        copy.wait()
    for d in range(1, ROWS):
        remote(c_own, c_all.at[me], in_send.at[0], in_recv.at[0], plane=peer(d)).start()
        remote(r_own.at[peer(d)], r_all.at[me], in_send.at[1], in_recv.at[1], plane=peer(d)).start()
    c_all[me] = c_own[...]
    r_all[me] = r_own[me]
    for l in (0, 1):
        passes(l)
    for l in (4, 5):
        lines(l)
    for l in (2, 3):
        passes(l)
    for l in (6, 7):
        lines(l)
    others = c_all.at[pl.ds(0, PEERS)]
    pltpu.make_async_copy(others, others, in_recv.at[0]).wait()
    others = r_all.at[pl.ds(0, PEERS)]
    pltpu.make_async_copy(others, others, in_recv.at[1]).wait()
    def extras():
        return [remote(src, dst, e_send.at[k], e_recv.at[k], layer=partner)
                for k, (src, dst) in enumerate(((r_all, r2_all), (c_all, c2_all), (len_own, len2)))]

    @pl.when(helper)
    def _():
        len_own[...] = jnp.full(len_own.shape, live, jnp.int32)
        for copy in extras():
            copy.start()

    for l in (4, 5):
        passes(l)

    @pl.when(worker)
    def _():
        for copy in extras():
            copy.wait_recv()
        for i in range(ROWS):
            for l in range(LEVELS):
                right[l, i] = r_all[i, l].astype(jnp.float32)
                couple[l, i] = jnp.broadcast_to(c_all[i, l:l + 1], couple.shape[2:])
                right[LEVELS + l, i] = r2_all[i, l].astype(jnp.float32)
                couple[LEVELS + l, i] = jnp.broadcast_to(c2_all[i, l:l + 1], couple.shape[2:])

    for l in (6, 7):
        passes(l)

    tile = r_all.shape[2:]

    def pair(l, i, field):
        zero = jnp.zeros(tile, jnp.float32)
        before, here, there, after = [field(j) if 0 <= j < ROWS else zero for j in range(i - 1, i + 3)]
        store, l = (wall, l) if l < LEVELS else (wall2, l - LEVELS)
        left, right_ = store.at[l, i // SIDE, i % SIDE], store.at[l, (i + 1) // SIDE, (i + 1) % SIDE]
        centre = jnp.dot(
            jnp.concatenate([here, there], axis=1).astype(jnp.bfloat16),
            jnp.concatenate([left[BS:], right_[:2 * BS]], axis=1),
            preferred_element_type=jnp.float32)
        outer = jnp.concatenate(
            [jnp.concatenate([before, zero], axis=0), jnp.concatenate([zero, after], axis=0)], axis=1)
        outer = jnp.dot(
            outer.astype(jnp.bfloat16), jnp.concatenate([left[:BS], right_[2 * BS:]], axis=0),
            preferred_element_type=jnp.float32)
        half_ = tile[0]
        return centre[:, :BS] + outer[:half_], centre[:, BS:] + outer[half_:]

    def alive(l):
        return jnp.full(tile, live, jnp.int32) > l if l < LEVELS else len2[...] > l - LEVELS

    def chunk(ref, part):
        return ref.at[pl.ds(CHUNK * part, CHUNK)]

    def down_copy(part, where):
        return remote(chunk(down_out, part), chunk(down_in, part), hop_send.at[0, part], hop_recv.at[0, part], layer=where)

    def up_copy(part, where):
        return remote(chunk(up_out, part), chunk(up_in, part), hop_send.at[1, part], hop_recv.at[1, part], layer=where)

    def arrivals(copy, where, i):
        if i == 0:
            copy(0, where).wait_recv()
        part = (i + 2) // CHUNK
        if (i + 2) % CHUNK == 0 and part < ROWS // CHUNK:
            copy(part, where).wait_recv()

    def arrived(l):
        if l < LEVELS:
            for step in (1, -1):
                line_pass(l, step).wait_recv()
        else:
            for k in range(5):
                hand(l - LEVELS, k).wait_recv()

    def down(start):
        now = {}

        def operand(l, i):
            if l > 0:
                return right[l, i] + couple[l, i] * now[l - 1, i]
            if start:
                return right[l, i]
            return right[l, i] + couple[l, i] * down_in[i].astype(jnp.float32)

        for l in range(2 * LEVELS):
            if start:
                arrived(l)
            keep = alive(l)
            made = {}

            def field(i):
                if i not in made:
                    made[i] = operand(l, i)
                return made[i]

            for i in range(0, ROWS, 2):
                if l == 0 and not start:
                    arrivals(down_copy, s - 2, i)
                for j, value in zip((i, i + 1), pair(l, i, field)):
                    vals[l, j] = value
                    if l > 0:
                        value = jnp.where(keep, value, now[l - 1, j])
                    now[l, j] = value
                if l == 2 * LEVELS - 1:
                    for j in (i, i + 1):
                        down_out[j] = now[l, j].astype(jnp.bfloat16)
                    if (i + 2) % CHUNK == 0:
                        if start:
                            down_copy(i // CHUNK, s + 2).start()
                        else:
                            @pl.when(jnp.logical_not(last))
                            def _(part=i // CHUNK):
                                down_copy(part, s + 2).start()

    def out_copy(d, low, high):
        part = pl.ds(low, high - low)
        return remote(o_all.at[part, peer(d)], o_ref.at[part, me], out_send, out_recv, plane=peer(d))

    def out_sends2():
        for d in range(ROWS):
            remote(o_all.at[pl.ds(LEVELS, LEVELS), peer(d)], o_ref.at[:, me], out_send2, out_recv,
                   layer=s + 1, plane=peer(d)).start()

    def out_sends(low, high):
        for d in range(1, ROWS):
            out_copy(d, low, high).start()

    def up(start, end):
        now = {}

        def field_at(l, i):
            return now[l + 1, i] if l < 2 * LEVELS - 1 else up_in[i].astype(jnp.float32)

        for l in reversed(range(2 * LEVELS)):
            keep = alive(l)
            top = l == 2 * LEVELS - 1
            for i in range(0, ROWS, 2):
                if start and top:
                    sums = (0.0, 0.0)
                else:
                    if top:
                        arrivals(up_copy, s + 2, i)
                    sums = pair(l, i, lambda j: field_at(l, j))
                for j, total in zip((i, i + 1), sums):
                    answer = vals[l, j] + total
                    o_all[l, j] = jnp.where(keep, answer, 0.0).astype(jnp.bfloat16)
                    if l > 0 or not end:
                        behind = jnp.zeros(tile, jnp.float32) if start and top else field_at(l, j)
                        now[l, j] = jnp.where(keep, couple[l, j] * answer, behind)
                if l == 0 and not end:
                    for j in (i, i + 1):
                        up_out[j] = now[l, j].astype(jnp.bfloat16)
                    if (i + 2) % CHUNK == 0:
                        up_copy(i // CHUNK, s - 2).start()
            if end and l == LEVELS:
                out_sends2()
            if end and l == 4:
                out_sends(4, 8)
            if end and l == 1:
                out_sends(1, 4)
        if end:
            out_sends(0, 1)
        else:
            out_sends2()
            out_sends(0, LEVELS)

    @pl.when(helper)
    def _():
        for l in range(LEVELS):
            for step in (1, -1):
                line_pass(l, step).wait_recv()
                hand(l, 3 if step == 1 else 4).start()

    @pl.when(first)
    def _():
        down(True)

    @pl.when(jnp.logical_and(worker, jnp.logical_not(first)))
    def _():
        for l in range(2 * LEVELS):
            arrived(l)
        down(False)

    @pl.when(last)
    def _():
        up(True, False)

    @pl.when(jnp.logical_and(worker, jnp.logical_and(jnp.logical_not(first), jnp.logical_not(last))))
    def _():
        up(False, False)

    @pl.when(first)
    def _():
        up(False, True)

    for l in range(LEVELS):
        for step in (1, -1):
            for send in (own_send, own_pass, line_send, line_pass):
                send(l, step).wait_send()
    others = c_all.at[pl.ds(0, PEERS)]
    pltpu.make_async_copy(others, others, in_send.at[0]).wait()
    others = r_all.at[pl.ds(0, PEERS)]
    pltpu.make_async_copy(others, others, in_send.at[1]).wait()

    @pl.when(jnp.logical_and(worker, jnp.logical_not(last)))
    def _():
        down_copy(0, s + 2).wait_send()

    @pl.when(jnp.logical_and(worker, jnp.logical_not(first)))
    def _():
        up_copy(0, s - 2).wait_send()

    @pl.when(worker)
    def _():
        keep = pltpu.make_async_copy(o_all.at[pl.ds(0, LEVELS), me], o_ref.at[:, me], keep_sem)
        keep.start()
        others = o_all.at[pl.ds(0, LEVELS), pl.ds(0, PEERS)]
        pltpu.make_async_copy(others, others, out_send).wait()
        others = o_all.at[pl.ds(LEVELS, LEVELS)]
        pltpu.make_async_copy(others, others, out_send2).wait()
        keep.wait()
        others = o_ref.at[:, pl.ds(0, PEERS)]
        pltpu.make_async_copy(others, others, out_recv).wait()

    @pl.when(helper)
    def _():
        for l in range(LEVELS):
            for k in range(5):
                hand(l, k).wait_send()
        for copy in extras():
            copy.wait_send()
        pltpu.make_async_copy(o_ref, o_ref, out_recv).wait()


def sweep(lengths, index, right, coupling, blocks):
    levels, _, cols, _ = right.shape
    per_row = blocks.shape[2]
    smem = pl.BlockSpec(memory_space=pltpu.SMEM)
    hbm = pl.BlockSpec(memory_space=pl.ANY)
    field = pltpu.VMEM((ROWS, cols, BS), jnp.bfloat16)
    stack = pltpu.VMEM((2 * levels, ROWS, cols, BS), jnp.bfloat16)
    inputs = pltpu.VMEM((ROWS, levels, cols, BS), jnp.bfloat16)
    wide = pltpu.VMEM((2 * levels, ROWS, cols, BS), jnp.float32)
    dma = pltpu.SemaphoreType.DMA
    return pl.pallas_call(
        sweep_kernel,
        in_specs=[smem, smem, hbm, hbm, hbm],
        out_specs=hbm,
        out_shape=jax.ShapeDtypeStruct(right.shape, jnp.bfloat16),
        scratch_shapes=[
            pltpu.VMEM((levels, per_row, BS, BS), jnp.bfloat16),
            pltpu.VMEM((levels, SIDE, SIDE, 3 * BS, BS), jnp.bfloat16),
            pltpu.VMEM((levels, SIDE, SIDE, 3 * BS, BS), jnp.bfloat16),
            inputs, inputs, inputs,
            pltpu.VMEM((levels, BS), jnp.float32),
            pltpu.VMEM((ROWS, levels, BS), jnp.float32),
            pltpu.VMEM((ROWS, levels, BS), jnp.float32),
            pltpu.VMEM((cols, BS), jnp.int32),
            pltpu.VMEM((cols, BS), jnp.int32),
            stack,
            wide, wide, wide,
            field, field, field, field,
            dma((levels,)), dma((levels + 1,)), dma((levels, 8)), dma((levels, 8)),
            dma((2,)), dma((2,)), dma, dma, dma((2, ROWS // CHUNK)), dma((2, ROWS // CHUNK)),
            pltpu.SemaphoreType.REGULAR((3,)), dma,
            dma((levels, 5)), dma((levels, 5)), dma((3,)), dma((3,)), dma,
        ],
        compiler_params=pltpu.CompilerParams(
            collective_id=0, has_side_effects=True, vmem_limit_bytes=57 * 1024 * 1024),
        name="sweep",
    )(lengths, index, right, coupling, blocks)


def on_device(right_sides, coupling, blocks, block_index, section_lengths):
    levels, columns, width = right_sides.shape
    right = right_sides.reshape(levels, ROWS, columns // ROWS, width)
    out = sweep(section_lengths, block_index, right, coupling, blocks)
    return out.reshape(levels, columns, width)


def solution(mesh):
    return jax.shard_map(
        on_device,
        mesh=mesh,
        in_specs=(
            P("layer", None, "plane"),
            P("layer", "plane"),
            P("layer", "plane", None, None, None),
            P("layer", "plane", None),
            P("layer"),
        ),
        out_specs=P("layer", None, "plane"),
        check_vma=False,
    )
```
